32 devices in a mesh: atoms: 32 (over z, y, x, core).
Axes of the slice: x: 2, y: 2, z: 4, core: 2. Of those that a mesh axis runs over, the one named last changes fastest.
Arguments:
- features: bfloat16 [4096, 9, 128], P('atoms'), may hold values from -6 to 6
- cotangent: bfloat16 [4096, 9, 128], P('atoms'), may hold values from -6 to 6
- wigner: float32 [9, 9, 12288], P(None, None, 'atoms'), may hold values from -1 to 1, as said below
- pair_blocks: int32 [512, 2], P('atoms'), may hold values from 0 to 31, all different within a row; in each aligned block of 16 rows (0 to 15, 16 to 31, ...) at most 2 rows name the same one
- pair_rows: int32 [2, 6, 512], P(None, None, 'atoms'), may hold values from 0 to 127
- edge_ends: int32 [2, 12288], P(None, 'atoms'), may hold values from 0 to 5
- first_m0: bfloat16 [768, 512], replicated, may hold values from -0.21875 to 0.21875
- first_m1: bfloat16 [2, 512, 256], replicated, may hold values from -0.1875 to 0.1875
- first_m2: bfloat16 [2, 256, 128], replicated, may hold values from -0.25 to 0.25
- second_m0: bfloat16 [384, 384], replicated, may hold values from -0.3125 to 0.3125
- second_m1: bfloat16 [2, 256, 256], replicated, may hold values from -0.25 to 0.25
- second_m2: bfloat16 [2, 128, 128], replicated, may hold values from -0.375 to 0.375
Outputs:
- messages: bfloat16 [4096, 9, 128], P('atoms')
- grad_features: float32 [4096, 9, 128], P('atoms')
- grad_first_m0: float32 [768, 512], replicated
- grad_first_m1: float32 [2, 512, 256], replicated
- grad_first_m2: float32 [2, 256, 128], replicated
- grad_second_m0: float32 [384, 384], replicated
- grad_second_m1: float32 [2, 256, 256], replicated
- grad_second_m2: float32 [2, 128, 128], replicated
The draws below stay inside these ranges and needn't reach their ends.
Inputs may be any that keep to these rules, and one draw needn't show every extreme that they name: `pair_blocks`: among the 16 pairs of one device no atom block is named more than 2 times; the two blocks of a pair differ. `wigner`: each edge's matrix is orthogonal and block diagonal over degrees 0, 1 and 2.
All inputs are finite; a program needn't handle non-finite values.
Results may differ from the reference program's by a relative error of at most 0.0045.
Values may be sent and summed in bfloat16 or wider, within the bound.
A program may use at most 128 MiB of HBM per device.

```python
import math
import jax
import jax.numpy as jnp
import numpy as np
from jax import lax

C = 128
COEF = 9
BLK = 128
RPP = 6
EPP = 24
PAIRS_DEV = 16
MOST = 2
ATOMS = 4096
PAIRS = 512
EDGES = 12288
N_ATOMS = 32


def quad_table():
    table = np.zeros((5, 3, 3), dtype=np.float32)
    root_half = 1.0 / np.sqrt(2.0)
    table[0, 0, 1] = root_half
    table[0, 1, 0] = root_half
    table[1, 1, 2] = root_half
    table[1, 2, 1] = root_half
    table[2, 0, 0] = -1.0 / np.sqrt(6.0)
    table[2, 1, 1] = -1.0 / np.sqrt(6.0)
    table[2, 2, 2] = 2.0 / np.sqrt(6.0)
    table[3, 0, 2] = root_half
    table[3, 2, 0] = root_half
    table[4, 0, 0] = root_half
    table[4, 1, 1] = -root_half
    return table


def draw_wigner(key, part):
    quaternion = jax.random.normal(key, (4, EDGES), jnp.float32)
    quaternion = quaternion / jnp.sqrt(jnp.sum(quaternion * quaternion, axis=0, keepdims=True) + 1e-12)
    qw = quaternion[0]
    qx = quaternion[1]
    qy = quaternion[2]
    qz = quaternion[3]
    rotation = jnp.stack([jnp.stack([1.0 - 2.0 * (qy * qy + qz * qz), 2.0 * (qx * qy - qz * qw), 2.0 * (qx * qz + qy * qw)]), jnp.stack([2.0 * (qx * qy + qz * qw), 1.0 - 2.0 * (qx * qx + qz * qz), 2.0 * (qy * qz - qx * qw)]), jnp.stack([2.0 * (qx * qz - qy * qw), 2.0 * (qy * qz + qx * qw), 1.0 - 2.0 * (qx * qx + qy * qy)])])
    axis_order = jnp.array([1, 2, 0], dtype=jnp.int32)
    first_degree = jnp.take(jnp.take(rotation, axis_order, axis=0), axis_order, axis=1)
    quad_basis = jnp.array(quad_table())
    second_degree = jnp.einsum('aij,jke,bkl,ile->abe', quad_basis, rotation, quad_basis, rotation)
    assembled = jnp.zeros((9, 9, EDGES), jnp.float32)
    assembled = assembled.at[0, 0].set(1.0)
    assembled = assembled.at[1:4, 1:4].set(first_degree)
    assembled = assembled.at[4:9, 4:9].set(second_degree)
    return assembled


def set_ends(result, stream_key, least, largest):
    longest = result.shape.index(max(result.shape))
    spots = []
    for shift in (0, 1):
        where = [jax.random.randint(jax.random.fold_in(stream_key, axis), (), 0, length) for axis, length in enumerate(result.shape)]
        where[longest] = (where[longest] + shift) % result.shape[longest]
        spots.append(tuple(where))
    return result.at[spots[0]].set(least).at[spots[1]].set(largest)


def levels(own_key, extent, pieces, low, high):
    gain = 1.0
    for axis_at, shards_of in pieces:
        draws = jax.random.uniform(jax.random.fold_in(jax.random.fold_in(own_key, 6), axis_at), (shards_of,), jnp.float32, low / len(pieces), high / len(pieces))
        gain = gain * jnp.repeat(jnp.exp(draws), extent[axis_at] // shards_of).reshape((-1,) + (1,) * (len(extent) - 1 - axis_at))
    return gain


def shared_out(own_key, own, number, rows, count, top, reach, slope):
    sequence = jax.random.permutation(own_key, count)
    crowded, common = load_shares(count, rows * top, reach, slope, True), load_shares(count, rows * top, reach, slope, False)
    places = jnp.arange(count)

    def named(sizes, turn):
        used = int((sizes > 0).sum())
        fixed = max(1, used // 4)
        passed = fixed + (places - fixed + turn * (used - fixed)) % max(1, count - fixed)
        return jnp.zeros((count,), jnp.int32).at[sequence[jnp.where(places < fixed, places, passed)]].set(jnp.asarray(sizes, jnp.int32))

    sizes = jnp.where(number % 4 == 0, named(crowded, number // 4), named(common, number - number // 4 - 1))
    mixed = jax.random.permutation(jax.random.fold_in(own, 3), count)
    donor, receiver = mixed[0:count // 2 * 2:2], mixed[1:count // 2 * 2:2]
    slack = jnp.minimum(sizes[donor] - 1, reach - sizes[receiver]) // 2
    slack = jnp.where((donor == sequence[0]) | (receiver == sequence[0]) | (sizes[receiver] == 0), 0, jnp.maximum(slack, 0))
    passed = jax.random.randint(jax.random.fold_in(own, 4), (count // 2,), 0, 1 << 20) % (slack + 1)
    sizes = sizes.at[donor].add(-passed).at[receiver].add(passed)
    members = jnp.searchsorted(jnp.cumsum(sizes), jnp.arange(rows * top), side="right").astype(jnp.int32)
    grid = members.reshape(top, rows).T
    grid = grid[jax.random.permutation(jax.random.fold_in(own, 1), rows)]
    turn = jax.random.randint(jax.random.fold_in(own, 2), (rows, 1), 0, top)
    return jnp.take_along_axis(grid, (jnp.arange(top)[None, :] + turn) % top, axis=1)


def load_shares(count, total, reach, lean, full):
    loads = [(1 << 20) // math.isqrt(grade ** lean) + 1 for grade in range(1, count + 1)]
    largest = reach if full else min(reach, max(-(-total // count), total * loads[0] // sum(loads)))
    least = 1 if total - largest >= count - 1 else 0
    given, rest = [largest] + [least] * (count - 1), total - largest - least * (count - 1)
    while rest > 0:
        free = [i for i in range(1, count) if given[i] < largest] or [i for i in range(1, count) if given[i] < reach]
        whole, remaining = sum([loads[i] for i in free]), rest
        for i in free:
            extra = min(reach - given[i], max(1, remaining * loads[i] // whole), rest)
            given[i] = given[i] + extra
            rest = rest - extra
    return np.array(given)


def noise(own_key, shape, spread, limit, split=(), held_as=jnp.bfloat16):
    level = levels(own_key, shape, split, -0.22, 0.18) if split else 1.0
    result = jax.random.normal(own_key, shape, jnp.float32) * spread * level
    return jnp.minimum(jnp.maximum(result, -limit), limit).astype(held_as)


def setup_inputs(seed: int = 0) -> dict:
    keys = jax.random.split(jax.random.key(seed), 13)
    features = noise(keys[0], (ATOMS, COEF, C), 1.0, 6.0, ((0, 32),))
    cotangent = noise(keys[1], (ATOMS, COEF, C), 1.0, 6.0, ((0, 32),))
    wigner = draw_wigner(jax.random.fold_in(keys[12], 71), 0)
    pair_blocks_keys = jax.random.split(jax.random.fold_in(keys[3], 1), PAIRS // PAIRS_DEV)
    pair_blocks_turns = jax.random.permutation(jax.random.fold_in(keys[3], 3), PAIRS // PAIRS_DEV)
    pair_blocks = jax.vmap(lambda own, number: shared_out(jax.random.fold_in(keys[3], 2), own, number, PAIRS_DEV, N_ATOMS, 2, MOST, 2))(pair_blocks_keys, pair_blocks_turns).reshape((PAIRS, 2))
    pair_rows = set_ends(jax.random.randint(keys[4], (2, RPP, PAIRS), 0, BLK), jax.random.fold_in(keys[4], 1), 0, BLK - 1).astype(jnp.int32)
    edge_ends = set_ends(jax.random.randint(keys[5], (2, EDGES), 0, RPP), jax.random.fold_in(keys[5], 1), 0, RPP - 1).astype(jnp.int32)
    first_m0 = noise(keys[6], (6 * C, 4 * C), (6 * C) ** -0.5, 0.21875)
    first_m1 = noise(keys[7], (2, 4 * C, 2 * C), (8 * C) ** -0.5, 0.1875)
    first_m2 = noise(keys[8], (2, 2 * C, C), (4 * C) ** -0.5, 0.25)
    second_m0 = noise(keys[9], (3 * C, 3 * C), (3 * C) ** -0.5, 0.3125)
    second_m1 = noise(keys[10], (2, 2 * C, 2 * C), (4 * C) ** -0.5, 0.25)
    second_m2 = noise(keys[11], (2, C, C), (2 * C) ** -0.5, 0.375)
    return {"features": features, "cotangent": cotangent, "wigner": wigner, "pair_blocks": pair_blocks, "pair_rows": pair_rows, "edge_ends": edge_ends, "first_m0": first_m0, "first_m1": first_m1, "first_m2": first_m2, "second_m0": second_m0, "second_m1": second_m1, "second_m2": second_m2}


COEF_ORDER = (0, 2, 6, 3, 7, 1, 5, 8, 4)


def rotate(turned, row_block):
    return jnp.einsum("ije,ejc->eic", turned, row_block.astype(jnp.float32), precision=lax.Precision.HIGHEST)


def unrotate(turned, row_block):
    return jnp.einsum("ije,eic->ejc", turned, row_block, precision=lax.Precision.HIGHEST)


def widen_pair(pair_weights):
    upper_half = jnp.concatenate([pair_weights[0], pair_weights[1]], axis=1)
    lower_half = jnp.concatenate([-pair_weights[1], pair_weights[0]], axis=1)
    return jnp.concatenate([upper_half, lower_half], axis=0)


def narrow(gradient):
    half_rows = gradient.shape[0] // 2
    half_cols = gradient.shape[1] // 2
    return jnp.stack([gradient[:half_rows, :half_cols] + gradient[half_rows:, half_cols:],
                      gradient[:half_rows, half_cols:] - gradient[half_rows:, :half_cols]])


def forward_dot(left_rows, weight):
    return jnp.dot(left_rows, weight, preferred_element_type=jnp.float32)


def backward_dot(gradient, weight):
    return lax.dot_general(gradient, weight, (((1,), (1,)), ((), ())), preferred_element_type=jnp.float32)


def weight_dot(left_rows, gradient):
    return lax.dot_general(left_rows, gradient, (((0,), (0,)), ((), ())), preferred_element_type=jnp.float32)


def forward_part(turned, source, target, weights):
    zero_a, big_one_a, big_two_a, zero_b, big_one_b, big_two_b = weights
    row_count = source.shape[0]
    channels = source.shape[2]
    rot_source = rotate(turned, source)
    rot_target = rotate(turned, target)
    lifted = jnp.concatenate([jnp.concatenate([rot_source, rot_target], axis=2),
                              jnp.concatenate([rot_target, rot_source], axis=2)], axis=0)
    lifted = lifted.astype(jnp.bfloat16).reshape(2 * row_count, 18 * channels)
    zero_part = lifted[:, :6 * channels]
    one_part = lifted[:, 6 * channels:14 * channels]
    two_part = lifted[:, 14 * channels:]
    first_out = forward_dot(zero_part, zero_a)
    hidden = jnp.concatenate([first_out[:, :3 * channels], forward_dot(one_part, big_one_a),
                              forward_dot(two_part, big_two_a)], axis=1)
    gate_value = jax.nn.sigmoid(first_out[:, 3 * channels:])
    scalar_part = hidden[:, :channels]
    gated_part = hidden[:, channels:].reshape(2 * row_count, 8, channels)
    activated = jnp.concatenate([jax.nn.silu(scalar_part),
                                 (gated_part * gate_value[:, None, :]).reshape(2 * row_count, 8 * channels)],
                                axis=1).astype(jnp.bfloat16)
    mixed_rows = jnp.concatenate([forward_dot(activated[:, :3 * channels], zero_b),
                                  forward_dot(activated[:, 3 * channels:7 * channels], big_one_b),
                                  forward_dot(activated[:, 7 * channels:], big_two_b)], axis=1)
    mixed_rows = mixed_rows.reshape(2 * row_count, 9, channels)
    stored = (zero_part, one_part, two_part, scalar_part, gated_part, gate_value, activated)
    return unrotate(turned, mixed_rows[:row_count]), unrotate(turned, mixed_rows[row_count:]), stored


def backward_part(turned, stored, grad_target_in, grad_source_in, weights):
    zero_a, big_one_a, big_two_a, zero_b, big_one_b, big_two_b = weights
    zero_part, one_part, two_part, scalar_part, gated_part, gate_value, activated = stored
    row_count = grad_target_in.shape[0]
    channels = grad_target_in.shape[2]
    all_rows = 2 * row_count
    grad_mix = jnp.concatenate([rotate(turned, grad_target_in), rotate(turned, grad_source_in)], axis=0)
    grad_mix = grad_mix.astype(jnp.bfloat16).reshape(all_rows, 9 * channels)
    mix_zero = grad_mix[:, :3 * channels]
    mix_one = grad_mix[:, 3 * channels:7 * channels]
    mix_two = grad_mix[:, 7 * channels:]
    grad_act = jnp.concatenate([backward_dot(mix_zero, zero_b), backward_dot(mix_one, big_one_b),
                                backward_dot(mix_two, big_two_b)], axis=1)
    terms_second = (weight_dot(activated[:, :3 * channels], mix_zero),
                    narrow(weight_dot(activated[:, 3 * channels:7 * channels], mix_one)),
                    narrow(weight_dot(activated[:, 7 * channels:], mix_two)))
    head_gate = jax.nn.sigmoid(scalar_part)
    grad_scalar = grad_act[:, :channels] * head_gate * (1.0 + scalar_part * (1.0 - head_gate))
    grad_gated = grad_act[:, channels:].reshape(all_rows, 8, channels)
    gated_grad = (grad_gated * gate_value[:, None, :]).reshape(all_rows, 8 * channels)
    grad_gate = jnp.sum(grad_gated * gated_part, axis=1) * gate_value * (1.0 - gate_value)
    grad_zero = jnp.concatenate([grad_scalar, gated_grad[:, :2 * channels], grad_gate], axis=1).astype(jnp.bfloat16)
    grad_one = gated_grad[:, 2 * channels:6 * channels].astype(jnp.bfloat16)
    grad_two = gated_grad[:, 6 * channels:].astype(jnp.bfloat16)
    grad_lifted = jnp.concatenate([backward_dot(grad_zero, zero_a), backward_dot(grad_one, big_one_a),
                                   backward_dot(grad_two, big_two_a)], axis=1).reshape(all_rows, 9, 2 * channels)
    terms_first = (weight_dot(zero_part, grad_zero), narrow(weight_dot(one_part, grad_one)),
                   narrow(weight_dot(two_part, grad_two)))
    front_grad = grad_lifted[:row_count]
    back_grad = grad_lifted[row_count:]
    grad_source = unrotate(turned, front_grad[:, :, :channels] + back_grad[:, :, channels:])
    grad_target = unrotate(turned, front_grad[:, :, channels:] + back_grad[:, :, :channels])
    return grad_source, grad_target, terms_first + terms_second


def reference(features, cotangent, wigner, pair_blocks, pair_rows, edge_ends,
              first_m0, first_m1, first_m2, second_m0, second_m1, second_m2):
    channels = features.shape[2]
    coef_count = features.shape[1]
    per_device = PAIRS_DEV * EPP
    weights = (first_m0, widen_pair(first_m1), widen_pair(first_m2),
               second_m0, widen_pair(second_m1), widen_pair(second_m2))
    index_order = jnp.array(COEF_ORDER, dtype=jnp.int32)
    plain_weights = (first_m0, first_m1, first_m2, second_m0, second_m1, second_m2)

    def one_device(running, block_index):
        summed_msgs, summed_grads, totals = running
        pairs_here = lax.dynamic_slice_in_dim(pair_blocks, block_index * PAIRS_DEV, PAIRS_DEV, 0)
        rows_here = lax.dynamic_slice_in_dim(pair_rows, block_index * PAIRS_DEV, PAIRS_DEV, 2)
        ends_here = lax.dynamic_slice_in_dim(edge_ends, block_index * per_device, per_device, 1)
        turned = jnp.take(lax.dynamic_slice_in_dim(wigner, block_index * per_device, per_device, 2),
                          index_order, axis=0)
        pair_of = jnp.arange(per_device, dtype=jnp.int32) // EPP
        target = pairs_here[pair_of, 0] * BLK + rows_here[0, ends_here[0], pair_of]
        source = pairs_here[pair_of, 1] * BLK + rows_here[1, ends_here[1], pair_of]
        to_target, to_source, stored = forward_part(turned, features[source], features[target], weights)
        grad_source, grad_target, grad_terms = backward_part(turned, stored, cotangent[target],
                                                             cotangent[source], weights)
        summed_msgs = summed_msgs.at[target].add(to_target).at[source].add(to_source)
        summed_grads = summed_grads.at[source].add(grad_source).at[target].add(grad_target)
        totals = tuple(left_term + right_term for left_term, right_term in zip(totals, grad_terms))
        return (summed_msgs, summed_grads, totals), None

    initial = (jnp.zeros((BLK * N_ATOMS, coef_count, channels), jnp.float32),
               jnp.zeros((BLK * N_ATOMS, coef_count, channels), jnp.float32),
               tuple(jnp.zeros(weight.shape, jnp.float32) for weight in plain_weights))
    (summed_msgs, summed_grads, totals), unused = lax.scan(one_device, initial,
                                                           jnp.arange(N_ATOMS, dtype=jnp.int32))
    grad_scale = (2.0 * EDGES) ** -0.5
    return (summed_msgs.astype(jnp.bfloat16), summed_grads, totals[0] * grad_scale, totals[1] * grad_scale,
            totals[2] * grad_scale, totals[3] * grad_scale, totals[4] * grad_scale, totals[5] * grad_scale)
```

```python
import jax
import jax.numpy as jnp
from jax import lax
from jax.experimental import pallas as pl
from jax.experimental.pallas import tpu as pltpu
from jax.sharding import PartitionSpec as P

COEF_ORDER = (0, 2, 6, 3, 7, 1, 5, 8, 4)
DEGREES = ((0, 1), (1, 4), (4, 9))
LANES = 128
TILE = 16
STREAMS = 4
AT_ONCE = 31
VMEM_BYTES = 66_000_000
MESH = pl.DeviceIdType.MESH
F32, BF16 = jnp.float32, jnp.bfloat16


def degree_of(index):
    for low, high in DEGREES:
        if low <= index < high:
            return range(low, high)


def dot_nn(left, right):
    return jnp.dot(left, right, preferred_element_type=F32)


def dot_nt(left, right):
    return lax.dot_general(left, right, (((1,), (1,)), ((), ())), preferred_element_type=F32)


def dot_tn(left, right):
    return lax.dot_general(left, right, (((0,), (0,)), ((), ())), preferred_element_type=F32)


def as_hot(hit):
    return hit.astype(F32).astype(BF16)


def tile_parts(coefs, width):
    tiles = -(-coefs * width // TILE)
    parts = []
    for t in range(tiles):
        first = TILE * t // width
        last = min((TILE * t + TILE - 1) // width, coefs - 1)
        assert last - first <= 1
        parts.append((first, last, TILE * t % width))
    return parts


def own_offsets(coefs, width):
    return [width * j % TILE for j in range(coefs)]


def unique(values):
    return sorted(set(values))


def widen_into(ref, pair_ref):
    rows, cols = pair_ref.shape[1], pair_ref.shape[2]
    ref[:rows, :cols] = pair_ref[0]
    ref[:rows, cols:] = pair_ref[1]
    ref[rows:, :cols] = (-pair_ref[1].astype(F32)).astype(BF16)
    ref[rows:, cols:] = pair_ref[0]


def spread_kernel(packed_ref, *out_refs):
    at = 0
    for ref in out_refs:
        views = [ref] if len(ref.shape) == 2 else [ref.at[0], ref.at[1]]
        for view in views:
            height, width = view.shape
            for col in range(0, width, LANES):
                view[:, col : col + LANES] = packed_ref[at : at + height, :].astype(F32)
                at += height


def main_kernel(width, pair_chunk, per_pair, grad_scale, peers, *refs):
    (
        req_ref, feat_ref, cot_ref, wig_ref, pos_ref, own_ref, fa0, fa1, fa2, sb0, sb1, sb2,
        msg_ref, grad_ref, fin,
        wa1, wa2, wb1, wb2,
        asked, hots, mine, send_f, send_c, recv_f, recv_c, back_m, back_g,
        pf, pc, am, ag,
        z, hid, gate_ref, act, dmix, dout, work, contrib,
        acc, snd, rcv,
        req_s, req_r, f_s, f_r, c_s, c_r, m_s, m_r, g_s, g_r, w_s, w_r,
    ) = refs
    shared = send_c is None
    send_c = send_f if shared else send_c
    C = LANES
    coefs, atoms, _ = feat_ref.shape
    half = coefs * C
    edges = wig_ref.shape[0]
    pair_rows = pf.shape[0]
    parts = tile_parts(coefs, width)
    starts = unique(p[2] for p in parts)
    offsets = own_offsets(coefs, width)
    kinds = unique(offsets)
    slots = peers * TILE
    me = lax.axis_index("atoms")

    barrier = pltpu.get_barrier_semaphore()

    def greet(k, carry):
        pl.semaphore_signal(barrier, inc=1, device_id=(lax.rem(me + k, peers),), device_id_type=MESH)
        return carry

    lax.fori_loop(1, peers, greet, 0)
    pl.semaphore_wait(barrier, peers - 1)

    def copies(source, target, send_sem, recv_sem):
        def at(k):
            to = lax.rem(me + k, peers)
            return pltpu.make_async_remote_copy(
                src_ref=source.at[to],
                dst_ref=target.at[me],
                send_sem=send_sem.at[k],
                recv_sem=recv_sem.at[k],
                device_id=(to,),
                device_id_type=MESH,
            )

        def start(first=1, last=peers):
            def go(k, carry):
                at(k).start()
                return carry

            lax.fori_loop(first, last, go, 0)

        def wait():
            def go(k, carry):
                at(k).wait()
                return carry

            lax.fori_loop(1, peers, go, 0)

        return start, wait

    start_req, wait_req = copies(req_ref, asked, req_s, req_r)
    start_req()
    asked[me] = req_ref[me]
    widen_into(wa1, fa1)
    widen_into(wa2, fa2)
    widen_into(wb1, sb1)
    widen_into(wb2, sb2)
    base = 0
    for m, off in enumerate(kinds):
        span = slots * (1 + (off + width - 1) // TILE)
        ids = lax.broadcasted_iota(jnp.int32, (pair_rows, span), 1)
        mine[:, base : base + span] = as_hot(own_ref[:, m : m + 1] == ids)
        base += span
    wait_req()

    rows_of = lax.broadcasted_iota(jnp.int32, (slots, peers), 0) // TILE
    chooser = as_hot(rows_of == lax.broadcasted_iota(jnp.int32, (slots, peers), 1))
    wanted = dot_nn(chooser, asked[...].reshape(peers, C).astype(BF16))
    lane = lax.broadcasted_iota(jnp.int32, (slots, C), 1)
    inner = lax.broadcasted_iota(jnp.int32, (slots, C), 0) % TILE
    atom_ids = lax.broadcasted_iota(jnp.int32, (slots, 2 * atoms), 1).astype(F32)
    for s in range(len(starts)):
        column = jnp.sum(jnp.where(lane == inner + s * TILE, wanted, 0.0), axis=1, keepdims=True)
        hots[s] = as_hot(column == atom_ids)

    def pick(block_ref, out_ref):
        for t, (first, last, start) in enumerate(parts):
            hot = hots.at[starts.index(start)]
            depth = (last - first + 1) * atoms
            table = block_ref[first : last + 1].reshape(depth, C)
            rows = dot_nn(hot[:, :depth], table).astype(BF16)
            out_ref[:, TILE * t : TILE * (t + 1), :] = rows.reshape(peers, TILE, C)

    start_f, wait_f = copies(send_f, recv_f, f_s, f_r)
    start_c, wait_c = copies(send_c, recv_c, c_s, c_r)
    pick(feat_ref, send_f)
    start_f()
    recv_f[me] = send_f[me]
    if shared:
        wait_f()
    pick(cot_ref, send_c)
    start_c()
    recv_c[me] = send_c[me]

    def own_hot(j):
        m = kinds.index(offsets[j])
        base = sum(slots * (1 + (off + width - 1) // TILE) for off in kinds[:m])
        tiles = 1 + (offsets[j] + width - 1) // TILE
        return base, tiles, width * j // TILE

    def gather(recv, out):
        for j in range(coefs):
            base, tiles, first = own_hot(j)
            total = None
            for h in range(tiles):
                hot = mine[:, base + h * slots : base + (h + 1) * slots]
                t = first + h
                rows = recv[:, TILE * t : TILE * (t + 1), :].reshape(slots, C)
                term = dot_nn(hot, rows)
                total = term if total is None else total + term
            out[:, j * C : (j + 1) * C] = total.astype(BF16)

    def scatter(sums, out):
        for t in range(len(parts)):
            total = None
            for j in range(parts[t][0], parts[t][1] + 1):
                base, tiles, first = own_hot(j)
                h = t - first
                assert 0 <= h < tiles
                hot = mine[:, base + h * slots : base + (h + 1) * slots]
                term = dot_tn(hot, sums[:, j * C : (j + 1) * C])
                total = term if total is None else total + term
            out[:, TILE * t : TILE * (t + 1), :] = total.astype(BF16).reshape(peers, TILE, C)

    chunk = pair_chunk * per_pair
    locals_ = pair_chunk * 2 * (pair_rows // (2 * (edges // per_pair)))
    T, S = slice(0, chunk), slice(chunk, 2 * chunk)

    def hot_of(index):
        span = pl.ds(pl.multiple_of(index * chunk, chunk), chunk)
        ids = lax.broadcasted_iota(jnp.int32, (chunk, locals_), 1)
        return jnp.concatenate(
            [as_hot(pos_ref[span, side : side + 1] == ids) for side in (0, 1)], axis=0
        )

    def table_of(ref, index):
        return ref.at[pl.ds(pl.multiple_of(index * locals_, locals_), locals_)]

    def entries(index):
        wig = wig_ref[pl.ds(pl.multiple_of(index * chunk, chunk), chunk), :]

        def entry(row, col):
            k = row * coefs + col
            return jnp.broadcast_to(wig[:, k : k + 1], (chunk, C))

        return entry

    def rotate(index, hot, table, put):
        rows = table_of(table, index)
        for c in range(0, half, 384):
            work[:, c : c + 384] = dot_nn(hot, rows[:, c : c + 384])
        entry = entries(index)
        for i, o in enumerate(COEF_ORDER):
            at_target = at_source = None
            for j in degree_of(o):
                w = entry(o, j)
                left = w * work[T, j * C : (j + 1) * C]
                right = w * work[S, j * C : (j + 1) * C]
                at_target = left if at_target is None else at_target + left
                at_source = right if at_source is None else at_source + right
            put(i, at_target.astype(BF16), at_source.astype(BF16))

    def unrotate(index, hot, take, out):
        entry = entries(index)
        for j in range(coefs):
            at_target = at_source = None
            for i, o in enumerate(COEF_ORDER):
                if o not in degree_of(j):
                    continue
                w = entry(o, j)
                left, right = take(i)
                left, right = w * left, w * right
                at_target = left if at_target is None else at_target + left
                at_source = right if at_source is None else at_source + right
            for row, value in ((0, at_target), (chunk, at_source)):
                contrib[row : row + chunk, j * C : (j + 1) * C] = value.astype(BF16)
        rows = table_of(out, index)
        for c in range(0, half, 384):
            rows[:, c : c + 384] = dot_tn(hot, contrib[:, c : c + 384]).astype(BF16)

    def all_rows(index):
        return pl.ds(pl.multiple_of(index * 2 * chunk, 2 * chunk), 2 * chunk)

    def forward(index, carry):
        hot = hot_of(index)
        zc, hc, gc, ac = (r.at[all_rows(index)] for r in (z, hid, gate_ref, act))

        def put(i, rt, rs):
            left = slice(2 * i * C, (2 * i + 1) * C)
            right = slice((2 * i + 1) * C, (2 * i + 2) * C)
            zc[T, left] = rs
            zc[T, right] = rt
            zc[S, left] = rt
            zc[S, right] = rs

        rotate(index, hot, pf, put)
        first = dot_nn(zc[:, : 6 * C], fa0[...])
        hc[:, : 3 * C] = first[:, : 3 * C]
        gc[...] = jax.nn.sigmoid(first[:, 3 * C :])
        hc[:, 3 * C : 7 * C] = dot_nn(zc[:, 6 * C : 14 * C], wa1[...])
        hc[:, 7 * C :] = dot_nn(zc[:, 14 * C :], wa2[...])
        gate = gc[...]
        h0 = hc[:, :C]
        ac[:, :C] = (h0 * jax.nn.sigmoid(h0)).astype(BF16)
        for k in range(1, 9):
            ac[:, k * C : (k + 1) * C] = (hc[:, k * C : (k + 1) * C] * gate).astype(BF16)
        work[:, : 3 * C] = dot_nn(ac[:, : 3 * C], sb0[...])
        work[:, 3 * C : 7 * C] = dot_nn(ac[:, 3 * C : 7 * C], wb1[...])
        work[:, 7 * C : 9 * C] = dot_nn(ac[:, 7 * C :], wb2[...])

        def take(i):
            col = slice(i * C, (i + 1) * C)
            return work[T, col], work[S, col]

        unrotate(index, hot, take, am)
        return carry

    def backward(index, carry):
        hot = hot_of(index)
        hc, gc, dc, oc = (r.at[all_rows(index)] for r in (hid, gate_ref, dmix, dout))

        def put(i, ct, cs):
            dc[T, i * C : (i + 1) * C] = ct
            dc[S, i * C : (i + 1) * C] = cs

        rotate(index, hot, pc, put)
        dact = work
        dact[:, : 3 * C] = dot_nt(dc[:, : 3 * C], sb0[...])
        dact[:, 3 * C : 7 * C] = dot_nt(dc[:, 3 * C : 7 * C], wb1[...])
        dact[:, 7 * C : 9 * C] = dot_nt(dc[:, 7 * C :], wb2[...])
        gate = gc[...]
        h0 = hc[:, :C]
        head = jax.nn.sigmoid(h0)
        oc[:, :C] = (dact[:, :C] * head * (1.0 + h0 * (1.0 - head))).astype(BF16)
        grad_gate = None
        for k in range(1, 9):
            d = dact[:, k * C : (k + 1) * C]
            term = d * hc[:, k * C : (k + 1) * C]
            grad_gate = term if grad_gate is None else grad_gate + term
            at = k * C if k < 3 else (k + 1) * C
            oc[:, at : at + C] = (d * gate).astype(BF16)
        oc[:, 3 * C : 4 * C] = (grad_gate * gate * (1.0 - gate)).astype(BF16)
        return carry

    def inputs_grad(index, carry):
        hot = hot_of(index)
        oc = dout.at[all_rows(index)]
        work[:, : 6 * C] = dot_nt(oc[:, : 4 * C], fa0[...])
        work[:, 6 * C : 14 * C] = dot_nt(oc[:, 4 * C : 8 * C], wa1[...])
        work[:, 14 * C :] = dot_nt(oc[:, 8 * C :], wa2[...])

        def take(i):
            left = slice(2 * i * C, (2 * i + 1) * C)
            right = slice((2 * i + 1) * C, (2 * i + 2) * C)
            return work[T, right] + work[S, left], work[T, left] + work[S, right]

        unrotate(index, hot, take, ag)
        return carry

    chunks = edges // chunk
    if not shared:
        wait_f()
    gather(recv_f, pf)
    lax.fori_loop(0, chunks, forward, 0)
    ret_m, ret_g = recv_f, recv_c
    start_m, wait_m = copies(ret_m, back_m, m_s, m_r)
    start_g, wait_g = copies(ret_g, back_g, g_s, g_r)
    scatter(am, ret_m)
    start_m()
    back_m[me] = ret_m[me]

    wait_c()
    gather(recv_c, pc)
    lax.fori_loop(0, chunks, backward, 0)

    at = 0

    def put(value):
        nonlocal at
        height = value.shape[0]
        for col in range(0, value.shape[1], C):
            acc[at // TILE : (at + height) // TILE] = value[:, col : col + C].reshape(height // TILE, TILE, C)
            at += height

    def weight_pair(left, right):
        rows, cols = left.shape[1] // 2, right.shape[1] // 2
        upper = dot_tn(left[:, :rows], right)
        lower = dot_tn(left[:, rows:], right)
        put(upper[:, :cols] + lower[:, cols:])
        put(upper[:, cols:] - lower[:, :cols])

    put(dot_tn(z[:, : 6 * C], dout[:, : 4 * C]))
    weight_pair(z[:, 6 * C : 14 * C], dout[:, 4 * C : 8 * C])
    weight_pair(z[:, 14 * C :], dout[:, 8 * C :])
    put(dot_tn(act[:, : 3 * C], dmix[:, : 3 * C]))
    weight_pair(act[:, 3 * C : 7 * C], dmix[:, 3 * C : 7 * C])
    weight_pair(act[:, 7 * C :], dmix[:, 7 * C :])
    blocks = acc.shape[0]
    if at < blocks * TILE:
        acc[at // TILE :] = jnp.zeros((blocks - at // TILE, TILE, C), F32)

    bits = peers.bit_length() - 1
    stream = blocks // STREAMS
    core = lax.rem(me, 2)
    strides = [2**b for b in range(bits)]
    if bits >= 3:
        strides[1] = 2 + 2 * core
        strides[2] = 4 - 2 * core
    low = [q * stream for q in range(STREAMS)]

    def w_copy(source, target, q, stage, stride):
        bit = lax.rem(me // stride, 2)
        return pltpu.make_async_remote_copy(
            src_ref=source,
            dst_ref=target,
            send_sem=w_s.at[stage * STREAMS + q],
            recv_sem=w_r.at[stage * STREAMS + q],
            device_id=(me + stride * (1 - 2 * bit),),
            device_id_type=MESH,
        )

    def halve_start(q, stage):
        size = stream >> (stage + 1)
        bit = lax.rem(me // strides[stage], 2)
        sent = low[q] + (1 - bit) * size
        low[q] = low[q] + bit * size
        snd[pl.ds(sent, size)] = acc[pl.ds(sent, size)].astype(BF16)
        landing = q * stream + stream - 2 * size
        copy = w_copy(snd.at[pl.ds(sent, size)], rcv.at[pl.ds(landing, size)], q, stage, strides[stage])
        copy.start()
        return copy, size, landing

    def halve_end(q, stage, state):
        copy, size, landing = state
        copy.wait()
        kept = pl.ds(low[q], size)
        total = acc[kept] + rcv[landing : landing + size].astype(F32)
        if stage == bits - 1:
            fin[kept] = (total * grad_scale).astype(BF16)
        else:
            acc[kept] = total

    def double_start(q, stage):
        size = stream >> (stage + 1)
        here = fin.at[pl.ds(low[q], size)]
        copy = w_copy(here, here, q, bits + stage, strides[stage])
        copy.start()
        return copy, size

    def double_end(q, stage, state):
        copy, size = state
        copy.wait()
        bit = lax.rem(me // strides[stage], 2)
        low[q] = low[q] - bit * size

    states = [halve_start(q, 0) for q in range(STREAMS)]

    def half_step(stage):
        for q in range(STREAMS):
            halve_end(q, stage, states[q])
            if stage + 1 < bits:
                states[q] = halve_start(q, stage + 1)
            else:
                states[q] = double_start(q, stage)
            send_some()

    def whole_step(stage):
        for q in range(STREAMS):
            double_end(q, stage, states[q])
            if stage:
                states[q] = double_start(q, stage - 1)
            send_some()

    sent = [0]

    def send_some():
        if sent[0]:
            last = min(peers, sent[0] + AT_ONCE * (peers - 1) // 31)
            start_g(sent[0], last)
            sent[0] = last

    for index in range(chunks):
        inputs_grad(index, 0)
        if index < bits - 1:
            half_step(index)
    scatter(ag, ret_g)
    back_g[me] = ret_g[me]
    sent[0] = 1
    send_some()
    for stage in range(min(chunks, bits - 1), bits):
        half_step(stage)

    def collect(back, out, dtype):
        for j in range(coefs):
            total = None
            for t, (first, last, start) in enumerate(parts):
                if not first <= j <= last:
                    continue
                hot = hots.at[starts.index(start)][:, (j - first) * atoms : (j - first + 1) * atoms]
                rows = back[:, TILE * t : TILE * (t + 1), :].reshape(slots, C)
                term = dot_tn(hot, rows)
                total = term if total is None else total + term
            out[j] = total.astype(dtype)

    stages = list(reversed(range(bits)))
    whole_step(stages[0])
    while sent[0] < peers:
        send_some()
    wait_m()
    collect(back_m, msg_ref, BF16)
    for stage in stages[1:]:
        whole_step(stage)
    wait_g()
    collect(back_g, grad_ref, F32)


def local(features, cotangent, wigner, pair_blocks, pair_rows, edge_ends, *weights):
    peers = lax.axis_size("atoms")
    atoms, coefs, channels = features.shape
    pair_count = pair_blocks.shape[0]
    row_width = pair_rows.shape[1]
    edges = edge_ends.shape[1]
    per_pair = edges // pair_count
    slot_count = max(2, 4 * pair_count // peers)
    width = slot_count * row_width
    half = coefs * channels
    bits = peers.bit_length() - 1

    owners = pair_blocks.reshape(2 * pair_count)
    spots = jnp.arange(2 * pair_count, dtype=jnp.int32)
    rank = jnp.sum(
        (owners[:, None] == owners[None, :]) & (spots[:, None] > spots[None, :]), axis=1
    ).astype(jnp.int32)
    end_rows = jnp.transpose(pair_rows, (2, 0, 1)).reshape(2 * pair_count, row_width)
    place = owners * slot_count + rank
    names = jnp.arange(peers * slot_count, dtype=jnp.int32)
    request = jnp.sum(
        jnp.where((place[None, :] == names[:, None])[:, :, None], end_rows[None], 0), axis=1
    ).astype(F32)
    request = request.reshape(peers, width)

    parts = tile_parts(coefs, width)
    starts = unique(p[2] for p in parts)
    pieces = []
    for start in starts:
        pieces.append(request[:, start:][:, :TILE])
        left = TILE - (width - start)
        if left > 0:
            pieces.append(request[:, :left] + float(atoms))
    asked = jnp.concatenate(pieces, axis=1)
    asked = jnp.pad(asked, ((0, 0), (0, LANES - asked.shape[1]))).reshape(peers, 1, LANES)

    kinds = unique(own_offsets(coefs, width))
    row_in_slot = rank[:, None] * row_width + jnp.arange(row_width, dtype=jnp.int32)[None, :]
    owned = []
    for off in kinds:
        at = row_in_slot + off
        owned.append((at // TILE) * (peers * TILE) + owners[:, None] * TILE + at % TILE)
    own = jnp.stack(owned, axis=-1).reshape(2 * pair_count * row_width, len(kinds))

    crowded = peers > 64
    pair_chunk = pair_count // (4 if crowded else 2)
    in_chunk = jnp.arange(edges, dtype=jnp.int32) // per_pair % pair_chunk * (2 * row_width)
    positions = jnp.transpose(edge_ends) + in_chunk[:, None]
    positions = positions + jnp.array([[0, row_width]], dtype=jnp.int32)
    wig = jnp.transpose(wigner.reshape(coefs * coefs, edges))

    total_rows = sum(w.size for w in weights) // LANES
    unit = TILE * peers * STREAMS
    packed_rows = -(-total_rows // unit) * unit
    rows = 2 * edges
    chunk_rows = 2 * pair_chunk * per_pair
    V, DMA = pltpu.VMEM, pltpu.SemaphoreType.DMA
    first_m0, first_m1, first_m2, second_m0, second_m1, second_m2 = weights
    wide = [(2 * w.shape[1], 2 * w.shape[2]) for w in (first_m1, first_m2, second_m1, second_m2)]
    slots = peers * TILE
    mine_width = sum(slots * (1 + (off + width - 1) // TILE) for off in kinds)
    block = (peers, TILE * len(parts), channels)
    end_count = 2 * pair_count * row_width
    packed_blocks = (packed_rows // TILE, TILE, LANES)
    scratch = [
        *[V(shape, BF16) for shape in wide],
        V((peers, 1, LANES), F32),
        V((len(starts), slots, 2 * atoms), BF16),
        V((end_count, mine_width), BF16),
        *[V(block, BF16) for _ in range(5 if crowded else 6)],
        *[V((end_count, half), BF16) for _ in range(4)],
        V((rows, 2 * half), BF16),
        V((rows, half), F32),
        V((rows, channels), F32),
        V((rows, half), BF16),
        V((rows, half), BF16),
        V((rows, half + channels), BF16),
        V((chunk_rows, 2 * half), F32),
        V((chunk_rows, half), BF16),
        V(packed_blocks, F32),
        V(packed_blocks, BF16),
        V(packed_blocks, BF16),
        *[DMA((peers,)) for _ in range(10)],
        DMA((2 * bits * STREAMS,)),
        DMA((2 * bits * STREAMS,)),
    ]
    whole = pl.BlockSpec(memory_space=pltpu.VMEM)
    first_block = 15 + 4 + 3
    grad_scale = (2.0 * edges * peers) ** (-0.5)

    def body(*refs):
        refs = list(refs)
        if crowded:
            refs.insert(first_block + 1, None)
        main_kernel(width, pair_chunk, per_pair, grad_scale, peers, *refs)

    operands = (
        asked, jnp.transpose(features, (1, 0, 2)), jnp.transpose(cotangent, (1, 0, 2)),
        wig, positions, own, *weights,
    )
    messages, grads, packed = pl.pallas_call(
        body,
        out_shape=[
            jax.ShapeDtypeStruct((coefs, atoms, channels), BF16),
            jax.ShapeDtypeStruct((coefs, atoms, channels), F32),
            jax.ShapeDtypeStruct(packed_blocks, BF16),
        ],
        in_specs=[whole] * len(operands),
        out_specs=[whole] * 3,
        scratch_shapes=scratch,
        compiler_params=pltpu.CompilerParams(
            collective_id=0, has_side_effects=True, vmem_limit_bytes=VMEM_BYTES
        ),
        name="edges",
    )(*operands)
    outs = pl.pallas_call(
        spread_kernel,
        out_shape=[jax.ShapeDtypeStruct(w.shape, F32) for w in weights],
        in_specs=[whole],
        out_specs=[whole] * len(weights),
        compiler_params=pltpu.CompilerParams(vmem_limit_bytes=VMEM_BYTES),
        name="spread",
    )(packed.reshape(packed_rows, LANES))
    return (jnp.transpose(messages, (1, 0, 2)), jnp.transpose(grads, (1, 0, 2)), *outs)


def solution(mesh):
    in_specs = (
        P("atoms", None, None),
        P("atoms", None, None),
        P(None, None, "atoms"),
        P("atoms", None),
        P(None, None, "atoms"),
        P(None, "atoms"),
        P(),
        P(),
        P(),
        P(),
        P(),
        P(),
    )
    out_specs = (P("atoms", None, None), P("atoms", None, None), P(), P(), P(), P(), P(), P())
    return jax.shard_map(local, mesh=mesh, in_specs=in_specs, out_specs=out_specs, check_vma=False)
```

```python
import jax
import jax.numpy as jnp
from jax import lax
from jax.experimental import pallas as pl
from jax.experimental.pallas import tpu as pltpu
from jax.sharding import PartitionSpec as P

COEF_ORDER = (0, 2, 6, 3, 7, 1, 5, 8, 4)
DEGREES = ((0, 1), (1, 4), (4, 9))
LANES = 128
TILE = 16
STREAMS = 8
SKEW = 0
PER_PIECE = 8
AT_ONCE = 1
PER_SEND = 1
PER_EVENT = 0
GROUPS = 2
M_FIRST = 31
M_PART = 4
VMEM_BYTES = 66_000_000
MESH = pl.DeviceIdType.MESH
F32, BF16 = jnp.float32, jnp.bfloat16


def degree_of(index):
    for low, high in DEGREES:
        if low <= index < high:
            return range(low, high)


def dot_nn(left, right):
    return jnp.dot(left, right, preferred_element_type=F32)


def dot_nt(left, right):
    return lax.dot_general(left, right, (((1,), (1,)), ((), ())), preferred_element_type=F32)


def dot_tn(left, right):
    return lax.dot_general(left, right, (((0,), (0,)), ((), ())), preferred_element_type=F32)


def as_hot(hit):
    return hit.astype(F32).astype(BF16)


def tile_parts(coefs, width):
    tiles = -(-coefs * width // TILE)
    parts = []
    for t in range(tiles):
        first = TILE * t // width
        last = min((TILE * t + TILE - 1) // width, coefs - 1)
        assert last - first <= 1
        parts.append((first, last, TILE * t % width))
    return parts


def own_offsets(coefs, width):
    return [width * j % TILE for j in range(coefs)]


def unique(values):
    return sorted(set(values))


def widen_into(ref, pair_ref):
    rows, cols = pair_ref.shape[1], pair_ref.shape[2]
    ref[:rows, :cols] = pair_ref[0]
    ref[:rows, cols:] = pair_ref[1]
    ref[rows:, :cols] = (-pair_ref[1].astype(F32)).astype(BF16)
    ref[rows:, cols:] = pair_ref[0]


def final_kernel(weight_count, packed_ref, messages_ref, grads_ref, *refs):
    messages_out, grads_out = refs[:2]
    outs = refs[2 : 2 + weight_count]
    staged = refs[2 + weight_count : 2 + 2 * weight_count]
    sems = refs[-1]
    pending = [
        pltpu.make_async_copy(messages_ref, messages_out, sems.at[0]),
        pltpu.make_async_copy(grads_ref, grads_out, sems.at[1]),
    ]
    for copy in pending:
        copy.start()
    at = 0
    for index, (ref, out) in enumerate(zip(staged, outs)):
        views = [ref] if len(ref.shape) == 2 else [ref.at[0], ref.at[1]]
        for view in views:
            height, width = view.shape
            for col in range(0, width, LANES):
                rows = packed_ref[at // TILE : (at + height) // TILE]
                view[:, col : col + LANES] = rows.reshape(height, LANES).astype(F32)
                at += height
        copy = pltpu.make_async_copy(ref, out, sems.at[2 + index])
        copy.start()
        pending.append(copy)
    for copy in pending:
        copy.wait()


def main_kernel(width, pair_chunk, per_pair, grad_scale, peers, streams, *refs):
    (
        feat_in, cot_in, wig_in, *weights_in,
        blocks_ref, pair_rows_ref, ends_ref,
        msg_ref, grad_ref, fin,
        feat_ref, cot_ref, wig_raw, fa0, fa1, fa2, sb0, sb1, sb2,
        wa1, wa2, wb1, wb2,
        req_ref, asked, hots, mine, wig_ref, pos_ref, send_f, send_c, recv_f, recv_c, back_m, back_g,
        pf, pc, am, ag,
        z, hid, gate_ref, act, dmix, dout, work, contrib,
        acc, snd, rcv,
        in_s, req_s, req_r, f_s, f_r, c_s, c_r, m_s, m_r, g_s, g_r, w_s, w_r,
    ) = refs
    shared = send_c is None
    send_c = send_f if shared else send_c
    loads = [
        pltpu.make_async_copy(source, target, in_s.at[i])
        for i, (source, target) in enumerate(
            zip(
                (feat_in, cot_in, wig_in, *weights_in),
                (feat_ref, cot_ref, wig_raw, fa0, fa1, fa2, sb0, sb1, sb2),
            )
        )
    ]
    for load in loads:
        load.start()
    C = LANES
    coefs, atoms, _ = feat_ref.shape
    half = coefs * C
    edges = wig_raw.shape[2]
    pair_rows = pf.shape[0]
    parts = tile_parts(coefs, width)
    starts = unique(p[2] for p in parts)
    offsets = own_offsets(coefs, width)
    kinds = unique(offsets)
    slots = peers * TILE
    me = lax.axis_index("atoms")

    barrier = pltpu.get_barrier_semaphore()

    def greet(k, carry):
        pl.semaphore_signal(barrier, inc=1, device_id=(lax.rem(me + k, peers),), device_id_type=MESH)
        return carry

    lax.fori_loop(1, peers, greet, 0)

    pairs = blocks_ref.shape[1]
    row_width = pair_rows_ref.shape[0]
    ranks = width // row_width
    owners = blocks_ref[...].astype(F32)
    earlier = lax.broadcasted_iota(jnp.int32, (pairs, pairs), 0) < lax.broadcasted_iota(
        jnp.int32, (pairs, pairs), 1
    )
    peer_ids = lax.broadcasted_iota(jnp.int32, (peers, pairs), 0).astype(F32)
    owned = [(peer_ids == owners[side : side + 1]).astype(F32) for side in (0, 1)]
    count = dot_nn((owned[0] + owned[1]).astype(BF16), as_hot(earlier))
    lane = lax.broadcasted_iota(jnp.int32, (row_width, C), 1)
    member = lax.broadcasted_iota(jnp.int32, (row_width, C), 0)

    def wanted_row(lanes):
        flat = lanes % TILE
        for s, start in enumerate(starts):
            flat = jnp.where(lanes // TILE == s, flat + start, flat)
        later = flat >= width
        return jnp.where(later, flat - width, flat), later

    row_at, _ = wanted_row(lane)
    lanes_all = lax.broadcasted_iota(jnp.int32, (peers, C), 1)
    _, second = wanted_row(lanes_all)
    request = jnp.where(second, float(atoms), 0.0)
    for k in range(ranks):
        choose = as_hot((row_at == member + k * row_width) & (lane < TILE * len(starts)))
        for side in (0, 1):
            rows = dot_tn(pair_rows_ref[:, side, :].astype(F32).astype(BF16), choose)
            holder = jnp.where(count == float(k), owned[side], 0.0)
            request = request + dot_nn(holder.astype(BF16), rows.astype(BF16))
    req_ref[...] = request.reshape(peers, 1, C)

    pl.semaphore_wait(barrier, peers - 1)

    def copies(source, target, send_sem, recv_sem):
        def at(k):
            to = lax.rem(me + k, peers)
            return pltpu.make_async_remote_copy(
                src_ref=source.at[to],
                dst_ref=target.at[me],
                send_sem=send_sem.at[k],
                recv_sem=recv_sem.at[k],
                device_id=(to,),
                device_id_type=MESH,
            )

        def start(first=1, last=peers):
            def go(k, carry):
                at(k).start()
                return carry

            lax.fori_loop(first, last, go, 0)

        def wait():
            def go(k, carry):
                at(k).wait()
                return carry

            lax.fori_loop(1, peers, go, 0)

        return start, wait

    start_req, wait_req = copies(req_ref, asked, req_s, req_r)
    start_req()
    asked[me] = req_ref[me]
    wait_req()

    rows_of = lax.broadcasted_iota(jnp.int32, (slots, peers), 0) // TILE
    chooser = as_hot(rows_of == lax.broadcasted_iota(jnp.int32, (slots, peers), 1))
    wanted = dot_nn(chooser, asked[...].reshape(peers, C).astype(BF16))
    slot_lane = lax.broadcasted_iota(jnp.int32, (slots, C), 1)
    inner = lax.broadcasted_iota(jnp.int32, (slots, C), 0) % TILE
    atom_ids = lax.broadcasted_iota(jnp.int32, (slots, 2 * atoms), 1).astype(F32)
    for s in range(len(starts)):
        column = jnp.sum(jnp.where(slot_lane == inner + s * TILE, wanted, 0.0), axis=1, keepdims=True)
        hots[s] = as_hot(column == atom_ids)

    def pick(block_ref, out_ref):
        for t, (first, last, start) in enumerate(parts):
            hot = hots.at[starts.index(start)]
            depth = (last - first + 1) * atoms
            table = block_ref[first : last + 1].reshape(depth, C)
            rows = dot_nn(hot[:, :depth], table).astype(BF16)
            out_ref[:, TILE * t : TILE * (t + 1), :] = rows.reshape(peers, TILE, C)

    start_f, wait_f = copies(send_f, recv_f, f_s, f_r)
    start_c, wait_c = copies(send_c, recv_c, c_s, c_r)
    loads[0].wait()
    pick(feat_ref, send_f)
    start_f()
    recv_f[me] = send_f[me]
    if shared:
        wait_f()
    loads[1].wait()
    pick(cot_ref, send_c)
    start_c()
    recv_c[me] = send_c[me]

    own = None
    end_row = lax.broadcasted_iota(jnp.int32, (pair_rows, pairs), 0)
    first_row = lax.broadcasted_iota(jnp.int32, (pair_rows, pairs), 1) * (2 * row_width)
    row_ids = lax.broadcasted_iota(jnp.int32, (8, pairs), 0)
    for side in (0, 1):
        low = first_row + side * row_width
        inside = (end_row >= low) & (end_row < low + row_width)
        shift = jnp.where(inside, end_row - low, 0)
        held = jnp.sum(owned[side] * count, axis=0, keepdims=True)
        known = jnp.where(row_ids == 0, owners[side : side + 1], jnp.where(row_ids == 1, held, 0.0))
        known = jnp.where(row_ids == 2, 1.0, known)
        term = lax.dot_general(
            as_hot(inside), known.astype(BF16), (((1,), (1,)), ((), ())), preferred_element_type=F32
        )
        term = jnp.concatenate(
            [term[:, :2], jnp.sum(shift.astype(F32), axis=1, keepdims=True)], axis=1
        )
        own = term if own is None else own + term
    in_slot = own[:, 1:2] * float(row_width) + own[:, 2:3]
    base = 0
    for off in kinds:
        tiles = 1 + (off + width - 1) // TILE
        place = in_slot + float(off)
        place = jnp.where(place >= float(TILE), place + float(slots - TILE), place)
        place = place + own[:, 0:1] * float(TILE)
        ids = lax.broadcasted_iota(jnp.int32, (pair_rows, tiles * slots), 1).astype(F32)
        mine[:, base : base + tiles * slots] = as_hot(place == ids)
        base += tiles * slots

    for load in loads[2:]:
        load.wait()
    diagonal = lax.broadcasted_iota(jnp.int32, (edges, edges), 0) == lax.broadcasted_iota(
        jnp.int32, (edges, edges), 1
    )
    unit = diagonal.astype(F32)
    for i in range(coefs):
        turned = lax.dot_general(
            unit, wig_raw[i], (((1,), (1,)), ((), ())),
            precision=lax.Precision.HIGHEST, preferred_element_type=F32,
        )
        wig_ref[:, i * coefs : (i + 1) * coefs] = turned
    ends = lax.dot_general(
        as_hot(diagonal), ends_ref[...].astype(F32).astype(BF16), (((1,), (1,)), ((), ())),
        preferred_element_type=F32,
    )
    pair_base = None
    edge_ids = lax.broadcasted_iota(jnp.int32, (edges, 1), 0)
    for p in range(edges // per_pair):
        step = jnp.where(edge_ids >= p * per_pair, float(2 * row_width), 0.0)
        if p and p % pair_chunk == 0:
            step = jnp.where(edge_ids >= p * per_pair, float(2 * row_width * (1 - pair_chunk)), 0.0)
        pair_base = jnp.zeros_like(step) if pair_base is None else pair_base + step
    pos_ref[...] = ends + pair_base + jnp.where(
        lax.broadcasted_iota(jnp.int32, (edges, 2), 1) == 1, float(row_width), 0.0
    )
    widen_into(wa1, fa1)
    widen_into(wa2, fa2)
    widen_into(wb1, sb1)
    widen_into(wb2, sb2)

    def own_hot(j):
        m = kinds.index(offsets[j])
        base = sum(slots * (1 + (off + width - 1) // TILE) for off in kinds[:m])
        tiles = 1 + (offsets[j] + width - 1) // TILE
        return base, tiles, width * j // TILE

    def gather(recv, out):
        for j in range(coefs):
            base, tiles, first = own_hot(j)
            total = None
            for h in range(tiles):
                hot = mine[:, base + h * slots : base + (h + 1) * slots]
                t = first + h
                rows = recv[:, TILE * t : TILE * (t + 1), :].reshape(slots, C)
                term = dot_nn(hot, rows)
                total = term if total is None else total + term
            out[:, j * C : (j + 1) * C] = total.astype(BF16)

    def scatter(sums, out):
        for t in range(len(parts)):
            total = None
            for j in range(parts[t][0], parts[t][1] + 1):
                base, tiles, first = own_hot(j)
                h = t - first
                assert 0 <= h < tiles
                hot = mine[:, base + h * slots : base + (h + 1) * slots]
                term = dot_tn(hot, sums[:, j * C : (j + 1) * C])
                total = term if total is None else total + term
            out[:, TILE * t : TILE * (t + 1), :] = total.astype(BF16).reshape(peers, TILE, C)

    chunk = pair_chunk * per_pair
    locals_ = pair_chunk * 2 * (pair_rows // (2 * (edges // per_pair)))
    T, S = slice(0, chunk), slice(chunk, 2 * chunk)

    def hot_of(index):
        span = pl.ds(pl.multiple_of(index * chunk, chunk), chunk)
        ids = lax.broadcasted_iota(jnp.int32, (chunk, locals_), 1).astype(F32)
        return jnp.concatenate(
            [as_hot(pos_ref[span, side : side + 1] == ids) for side in (0, 1)], axis=0
        )

    def table_of(ref, index):
        return ref.at[pl.ds(pl.multiple_of(index * locals_, locals_), locals_)]

    def entries(index):
        wig = wig_ref[pl.ds(pl.multiple_of(index * chunk, chunk), chunk), :]

        def entry(row, col):
            k = row * coefs + col
            return jnp.broadcast_to(wig[:, k : k + 1], (chunk, C))

        return entry

    def rotate(index, hot, table, put):
        rows = table_of(table, index)
        for c in range(0, half, 384):
            work[:, c : c + 384] = dot_nn(hot, rows[:, c : c + 384])
        entry = entries(index)
        for i, o in enumerate(COEF_ORDER):
            at_target = at_source = None
            for j in degree_of(o):
                w = entry(o, j)
                left = w * work[T, j * C : (j + 1) * C]
                right = w * work[S, j * C : (j + 1) * C]
                at_target = left if at_target is None else at_target + left
                at_source = right if at_source is None else at_source + right
            put(i, at_target.astype(BF16), at_source.astype(BF16))

    def unrotate(index, hot, take, out):
        entry = entries(index)
        for j in range(coefs):
            at_target = at_source = None
            for i, o in enumerate(COEF_ORDER):
                if o not in degree_of(j):
                    continue
                w = entry(o, j)
                left, right = take(i)
                left, right = w * left, w * right
                at_target = left if at_target is None else at_target + left
                at_source = right if at_source is None else at_source + right
            for row, value in ((0, at_target), (chunk, at_source)):
                contrib[row : row + chunk, j * C : (j + 1) * C] = value.astype(BF16)
        rows = table_of(out, index)
        for c in range(0, half, 384):
            rows[:, c : c + 384] = dot_tn(hot, contrib[:, c : c + 384]).astype(BF16)

    def all_rows(index):
        return pl.ds(pl.multiple_of(index * 2 * chunk, 2 * chunk), 2 * chunk)

    def forward(index, carry):
        hot = hot_of(index)
        zc, hc, gc, ac = (r.at[all_rows(index)] for r in (z, hid, gate_ref, act))

        def put(i, rt, rs):
            left = slice(2 * i * C, (2 * i + 1) * C)
            right = slice((2 * i + 1) * C, (2 * i + 2) * C)
            zc[T, left] = rs
            zc[T, right] = rt
            zc[S, left] = rt
            zc[S, right] = rs

        rotate(index, hot, pf, put)
        first = dot_nn(zc[:, : 6 * C], fa0[...])
        hc[:, : 3 * C] = first[:, : 3 * C]
        gc[...] = jax.nn.sigmoid(first[:, 3 * C :])
        hc[:, 3 * C : 7 * C] = dot_nn(zc[:, 6 * C : 14 * C], wa1[...])
        hc[:, 7 * C :] = dot_nn(zc[:, 14 * C :], wa2[...])
        gate = gc[...]
        h0 = hc[:, :C]
        ac[:, :C] = (h0 * jax.nn.sigmoid(h0)).astype(BF16)
        for k in range(1, 9):
            ac[:, k * C : (k + 1) * C] = (hc[:, k * C : (k + 1) * C] * gate).astype(BF16)
        work[:, : 3 * C] = dot_nn(ac[:, : 3 * C], sb0[...])
        work[:, 3 * C : 7 * C] = dot_nn(ac[:, 3 * C : 7 * C], wb1[...])
        work[:, 7 * C : 9 * C] = dot_nn(ac[:, 7 * C :], wb2[...])

        def take(i):
            col = slice(i * C, (i + 1) * C)
            return work[T, col], work[S, col]

        unrotate(index, hot, take, am)
        return carry

    def backward_first(index, carry):
        hot = hot_of(index)
        dc = dmix.at[all_rows(index)]

        def put(i, ct, cs):
            dc[T, i * C : (i + 1) * C] = ct
            dc[S, i * C : (i + 1) * C] = cs

        rotate(index, hot, pc, put)
        return carry

    def backward(index, carry):
        hc, gc, dc, oc = (r.at[all_rows(index)] for r in (hid, gate_ref, dmix, dout))
        dact = work
        dact[:, : 3 * C] = dot_nt(dc[:, : 3 * C], sb0[...])
        dact[:, 3 * C : 7 * C] = dot_nt(dc[:, 3 * C : 7 * C], wb1[...])
        dact[:, 7 * C : 9 * C] = dot_nt(dc[:, 7 * C :], wb2[...])
        gate = gc[...]
        h0 = hc[:, :C]
        head = jax.nn.sigmoid(h0)
        oc[:, :C] = (dact[:, :C] * head * (1.0 + h0 * (1.0 - head))).astype(BF16)
        grad_gate = None
        for k in range(1, 9):
            d = dact[:, k * C : (k + 1) * C]
            term = d * hc[:, k * C : (k + 1) * C]
            grad_gate = term if grad_gate is None else grad_gate + term
            at = k * C if k < 3 else (k + 1) * C
            oc[:, at : at + C] = (d * gate).astype(BF16)
        oc[:, 3 * C : 4 * C] = (grad_gate * gate * (1.0 - gate)).astype(BF16)
        return carry

    def inputs_grad(index, carry):
        hot = hot_of(index)
        oc = dout.at[all_rows(index)]
        work[:, : 6 * C] = dot_nt(oc[:, : 4 * C], fa0[...])
        work[:, 6 * C : 14 * C] = dot_nt(oc[:, 4 * C : 8 * C], wa1[...])
        work[:, 14 * C :] = dot_nt(oc[:, 8 * C :], wa2[...])
        advance(PER_PIECE)

        def take(i):
            left = slice(2 * i * C, (2 * i + 1) * C)
            right = slice((2 * i + 1) * C, (2 * i + 2) * C)
            return work[T, right] + work[S, left], work[T, left] + work[S, right]

        unrotate(index, hot, take, ag)
        return carry

    chunks = edges // chunk
    if not shared:
        wait_f()
    gather(recv_f, pf)
    lax.fori_loop(0, chunks, forward, 0)
    ret_m, ret_g = recv_f, recv_c
    start_m, wait_m = copies(ret_m, back_m, m_s, m_r)
    start_g, wait_g = copies(ret_g, back_g, g_s, g_r)
    scatter(am, ret_m)
    back_m[me] = ret_m[me]
    returns = [(start, k) for start in (start_m, start_g) for k in range(1, peers)]
    grads_ready = [False]
    portion = max(1, (peers - 1) // 31)

    def give(number):
        number *= portion
        while number > 0 and returns:
            start, first = returns[0]
            if start is start_g and not grads_ready[0]:
                return
            last = first
            while returns and returns[0][0] is start and last - first < number:
                last = returns.pop(0)[1] + 1
            start(first, last)
            number -= last - first

    give(M_FIRST)

    wait_c()
    give(M_PART)
    gather(recv_c, pc)
    lax.fori_loop(0, chunks, backward_first, 0)
    give(M_PART)

    blocks = acc.shape[0]
    bits = peers.bit_length() - 1
    stream = blocks // streams
    core = lax.rem(me, 2)
    strides = [2**b for b in range(bits)]
    if bits >= 3:
        strides[1] = 2 + 2 * core
        strides[2] = 4 - 2 * core
    low = [q * stream for q in range(streams)]

    def w_copy(source, target, q, stage, stride):
        bit = lax.rem(me // stride, 2)
        return pltpu.make_async_remote_copy(
            src_ref=source,
            dst_ref=target,
            send_sem=w_s.at[stage * streams + q],
            recv_sem=w_r.at[stage * streams + q],
            device_id=(me + stride * (1 - 2 * bit),),
            device_id_type=MESH,
        )

    def halve_start(q, stage):
        size = stream >> (stage + 1)
        bit = lax.rem(me // strides[stage], 2)
        sent = low[q] + (1 - bit) * size
        low[q] = low[q] + bit * size
        snd[pl.ds(sent, size)] = acc[pl.ds(sent, size)].astype(BF16)
        landing = q * stream + stream - 2 * size
        copy = w_copy(snd.at[pl.ds(sent, size)], rcv.at[pl.ds(landing, size)], q, stage, strides[stage])
        copy.start()
        return copy, size, landing

    def halve_end(q, stage, state):
        copy, size, landing = state
        copy.wait()
        kept = pl.ds(low[q], size)
        total = acc[kept] + rcv[landing : landing + size].astype(F32)
        if stage == bits - 1:
            fin[kept] = (total * grad_scale).astype(BF16)
        else:
            acc[kept] = total

    def double_start(q, stage):
        size = stream >> (stage + 1)
        here = fin.at[pl.ds(low[q], size)]
        copy = w_copy(here, here, q, bits + stage, strides[stage])
        copy.start()
        return copy, size

    def double_end(q, stage, state):
        copy, size = state
        copy.wait()
        bit = lax.rem(me // strides[stage], 2)
        low[q] = low[q] - bit * size

    states = [None] * streams
    events = sorted(
        ((q * GROUPS // streams * SKEW + s, q, s) for q in range(streams) for s in range(2 * bits)), reverse=True
    )

    def step(q, s):
        if s < bits:
            halve_end(q, s, states[q])
            states[q] = halve_start(q, s + 1) if s + 1 < bits else double_start(q, s)
        else:
            stage = 2 * bits - 1 - s
            double_end(q, stage, states[q])
            if stage:
                states[q] = double_start(q, stage - 1)

    started = [0]

    def advance(number):
        for _ in range(number):
            if events and events[-1][1] < started[0]:
                _, q, s = events.pop()
                step(q, s)
                give(PER_EVENT)

    at = 0

    def put(value):
        nonlocal at
        height = value.shape[0]
        for col in range(0, value.shape[1], C):
            acc[at // TILE : (at + height) // TILE] = value[:, col : col + C].reshape(height // TILE, TILE, C)
            at += height
        begin()

    def begin():
        while started[0] < streams and (started[0] + 1) * stream * TILE <= at:
            states[started[0]] = halve_start(started[0], 0)
            started[0] += 1

    def weight_pair(left, right):
        rows, cols = left.shape[1] // 2, right.shape[1] // 2
        upper = dot_tn(left[:, :rows], right)
        lower = dot_tn(left[:, rows:], right)
        put(upper[:, :cols] + lower[:, cols:])
        put(upper[:, cols:] - lower[:, :cols])

    put(dot_tn(act[:, : 3 * C], dmix[:, : 3 * C]))
    weight_pair(act[:, 3 * C : 7 * C], dmix[:, 3 * C : 7 * C])
    weight_pair(act[:, 7 * C :], dmix[:, 7 * C :])
    give(M_PART)
    lax.fori_loop(0, chunks, backward, 0)
    give(M_PART)
    put(dot_tn(z[:, : 6 * C], dout[:, : 4 * C]))
    advance(PER_PIECE)
    weight_pair(z[:, 6 * C : 14 * C], dout[:, 4 * C : 8 * C])
    advance(PER_PIECE)
    weight_pair(z[:, 14 * C :], dout[:, 8 * C :])
    if at < blocks * TILE:
        acc[at // TILE :] = jnp.zeros((blocks - at // TILE, TILE, C), F32)
        at = blocks * TILE
        begin()

    for index in range(chunks):
        inputs_grad(index, 0)
        advance(PER_PIECE)
    scatter(ag, ret_g)
    back_g[me] = ret_g[me]
    grads_ready[0] = True
    while returns:
        give(AT_ONCE)
        advance(PER_SEND)

    def collect(back, out, dtype):
        for j in range(coefs):
            total = None
            for t, (first, last, start) in enumerate(parts):
                if not first <= j <= last:
                    continue
                hot = hots.at[starts.index(start)][:, (j - first) * atoms : (j - first + 1) * atoms]
                rows = back[:, TILE * t : TILE * (t + 1), :].reshape(slots, C)
                term = dot_tn(hot, rows)
                total = term if total is None else total + term
            out[j] = total.astype(dtype)

    wait_m()
    collect(back_m, msg_ref, BF16)
    advance(len(events))
    wait_g()
    collect(back_g, grad_ref, F32)


def local(features, cotangent, wigner, pair_blocks, pair_rows, edge_ends, *weights):
    peers = lax.axis_size("atoms")
    atoms, coefs, channels = features.shape
    pair_count = pair_blocks.shape[0]
    row_width = pair_rows.shape[1]
    edges = edge_ends.shape[1]
    per_pair = edges // pair_count
    slot_count = max(2, 4 * pair_count // peers)
    width = slot_count * row_width
    half = coefs * channels
    bits = peers.bit_length() - 1

    parts = tile_parts(coefs, width)
    starts = unique(p[2] for p in parts)
    kinds = unique(own_offsets(coefs, width))
    crowded = peers > 64
    pair_chunk = pair_count // (4 if crowded else 2)
    total_rows = sum(w.size for w in weights) // LANES
    streams = 4 if crowded else STREAMS
    unit = TILE * peers * streams
    packed_rows = -(-total_rows // unit) * unit
    rows = 2 * edges
    chunk_rows = 2 * pair_chunk * per_pair
    V, DMA = pltpu.VMEM, pltpu.SemaphoreType.DMA
    first_m0, first_m1, first_m2, second_m0, second_m1, second_m2 = weights
    wide = [(2 * w.shape[1], 2 * w.shape[2]) for w in (first_m1, first_m2, second_m1, second_m2)]
    slots = peers * TILE
    mine_width = sum(slots * (1 + (off + width - 1) // TILE) for off in kinds)
    block = (peers, TILE * len(parts), channels)
    end_count = 2 * pair_count * row_width
    packed_blocks = (packed_rows // TILE, TILE, LANES)
    scratch = [
        V((coefs, atoms, channels), BF16),
        V((coefs, atoms, channels), BF16),
        V((coefs, coefs, edges), F32),
        *[V(w.shape, BF16) for w in weights],
        *[V(shape, BF16) for shape in wide],
        V((peers, 1, LANES), F32),
        V((peers, 1, LANES), F32),
        V((len(starts), slots, 2 * atoms), BF16),
        V((end_count, mine_width), BF16),
        V((edges, coefs * coefs), F32),
        V((edges, 2), F32),
        *[V(block, BF16) for _ in range(5 if crowded else 6)],
        *[V((end_count, half), BF16) for _ in range(4)],
        V((rows, 2 * half), BF16),
        V((rows, half), F32),
        V((rows, channels), F32),
        V((rows, half), BF16),
        V((rows, half), BF16),
        V((rows, half + channels), BF16),
        V((chunk_rows, 2 * half), F32),
        V((chunk_rows, half), BF16),
        V(packed_blocks, F32),
        V(packed_blocks, BF16),
        V(packed_blocks, BF16),
        DMA((3 + len(weights),)),
        *[DMA((peers,)) for _ in range(10)],
        DMA((2 * bits * streams,)),
        DMA((2 * bits * streams,)),
    ]
    whole = pl.BlockSpec(memory_space=pltpu.VMEM)
    first_block = 15 + 9 + 4 + 6
    grad_scale = (2.0 * edges * peers) ** (-0.5)

    def body(*refs):
        refs = list(refs)
        if crowded:
            refs.insert(first_block + 1, None)
        main_kernel(width, pair_chunk, per_pair, grad_scale, peers, streams, *refs)

    anywhere = pl.BlockSpec(memory_space=pl.ANY)
    messages, grads, packed = pl.pallas_call(
        body,
        out_shape=[
            jax.ShapeDtypeStruct((coefs, atoms, channels), BF16),
            jax.ShapeDtypeStruct((coefs, atoms, channels), F32),
            jax.ShapeDtypeStruct(packed_blocks, BF16),
        ],
        in_specs=[anywhere] * (3 + len(weights)) + [whole] * 3,
        out_specs=[whole] * 3,
        scratch_shapes=scratch,
        compiler_params=pltpu.CompilerParams(
            collective_id=0, has_side_effects=True, vmem_limit_bytes=VMEM_BYTES
        ),
        name="edges",
    )(
        jnp.transpose(features, (1, 0, 2)), jnp.transpose(cotangent, (1, 0, 2)), wigner, *weights,
        jnp.transpose(pair_blocks), jnp.transpose(pair_rows, (1, 0, 2)), edge_ends,
    )
    ordered = (second_m0, second_m1, second_m2, first_m0, first_m1, first_m2)

    def final(*refs):
        final_kernel(len(ordered), *refs)

    shapes = [jax.ShapeDtypeStruct(w.shape, F32) for w in ordered]
    messages, grads, *outs = pl.pallas_call(
        final,
        out_shape=[
            jax.ShapeDtypeStruct(messages.shape, BF16), jax.ShapeDtypeStruct(grads.shape, F32), *shapes
        ],
        in_specs=[whole] * 3,
        out_specs=[anywhere] * (2 + len(ordered)),
        scratch_shapes=[*[V(w.shape, F32) for w in ordered], DMA((2 + len(ordered),))],
        compiler_params=pltpu.CompilerParams(vmem_limit_bytes=VMEM_BYTES),
        name="finish",
    )(packed, messages, grads)
    outs = (*outs[3:], *outs[:3])
    return (jnp.transpose(messages, (1, 0, 2)), jnp.transpose(grads, (1, 0, 2)), *outs)


def solution(mesh):
    in_specs = (
        P("atoms", None, None),
        P("atoms", None, None),
        P(None, None, "atoms"),
        P("atoms", None),
        P(None, None, "atoms"),
        P(None, "atoms"),
        P(),
        P(),
        P(),
        P(),
        P(),
        P(),
    )
    out_specs = (P("atoms", None, None), P("atoms", None, None), P(), P(), P(), P(), P(), P())
    return jax.shard_map(local, mesh=mesh, in_specs=in_specs, out_specs=out_specs, check_vma=False)
```

```python
import jax
import jax.numpy as jnp
from jax import lax
from jax.experimental import pallas as pl
from jax.experimental.pallas import tpu as pltpu
from jax.sharding import PartitionSpec as P

COEF_ORDER = (0, 2, 6, 3, 7, 1, 5, 8, 4)
DEGREES = ((0, 1), (1, 4), (4, 9))
LANES = 128
TILE = 16
STREAMS = 8
STRIDE = 11
BEFORE = 0
SKEW = 0
PER_PIECE = 8
AT_ONCE = 1
PER_SEND = 1
PER_EVENT = 0
GROUPS = 2
M_FIRST = 31
M_PART = 4
VMEM_BYTES = 66_000_000
MESH = pl.DeviceIdType.MESH
F32, BF16 = jnp.float32, jnp.bfloat16


def degree_of(index):
    for low, high in DEGREES:
        if low <= index < high:
            return range(low, high)


def dot_nn(left, right):
    return jnp.dot(left, right, preferred_element_type=F32)


def dot_nt(left, right):
    return lax.dot_general(left, right, (((1,), (1,)), ((), ())), preferred_element_type=F32)


def dot_tn(left, right):
    return lax.dot_general(left, right, (((0,), (0,)), ((), ())), preferred_element_type=F32)


def as_hot(hit):
    return hit.astype(F32).astype(BF16)


def tile_parts(coefs, width):
    tiles = -(-coefs * width // TILE)
    parts = []
    for t in range(tiles):
        first = TILE * t // width
        last = min((TILE * t + TILE - 1) // width, coefs - 1)
        assert last - first <= 1
        parts.append((first, last, TILE * t % width))
    return parts


def own_offsets(coefs, width):
    return [width * j % TILE for j in range(coefs)]


def unique(values):
    return sorted(set(values))


def widen_into(ref, pair_ref):
    rows, cols = pair_ref.shape[1], pair_ref.shape[2]
    ref[:rows, :cols] = pair_ref[0]
    ref[:rows, cols:] = pair_ref[1]
    ref[rows:, :cols] = (-pair_ref[1].astype(F32)).astype(BF16)
    ref[rows:, cols:] = pair_ref[0]


def final_kernel(weight_count, packed_in, messages_ref, grads_ref, *refs):
    messages_out, grads_out = refs[:2]
    outs = refs[2 : 2 + weight_count]
    staged = refs[2 + weight_count : 2 + 2 * weight_count]
    packed_ref, sems = refs[-2:]
    loads = []
    at = 0
    for index, ref in enumerate(staged):
        blocks = ref.size // (TILE * LANES)
        span = pl.ds(at, blocks)
        loads.append(
            pltpu.make_async_copy(packed_in.at[span], packed_ref.at[span], sems.at[2 + weight_count + index])
        )
        loads[-1].start()
        at += blocks
    pending = [
        pltpu.make_async_copy(messages_ref, messages_out, sems.at[0]),
        pltpu.make_async_copy(grads_ref, grads_out, sems.at[1]),
    ]
    for copy in pending:
        copy.start()
    at = 0
    for index, (ref, out) in enumerate(zip(staged, outs)):
        loads[index].wait()
        views = [ref] if len(ref.shape) == 2 else [ref.at[0], ref.at[1]]
        for view in views:
            height, width = view.shape
            for col in range(0, width, LANES):
                rows = packed_ref[at // TILE : (at + height) // TILE]
                view[:, col : col + LANES] = rows.reshape(height, LANES).astype(F32)
                at += height
        copy = pltpu.make_async_copy(ref, out, sems.at[2 + index])
        copy.start()
        pending.append(copy)
    for copy in pending:
        copy.wait()


def main_kernel(width, pair_chunk, per_pair, grad_scale, peers, streams, *refs):
    (
        feat_in, cot_in, wig_in, *weights_in,
        blocks_ref, pair_rows_ref, ends_ref,
        msg_out, grad_out, fin_out,
        msg_ref, grad_ref, fin,
        feat_ref, cot_ref, wig_raw, fa0, fa1, fa2, sb0, sb1, sb2,
        wa1, wa2, wb1, wb2,
        req_ref, asked, hots, mine, wig_ref, pos_ref, send_f, send_c, recv_f, recv_c, back_m, back_g,
        pf, pc, am, ag,
        z, hid, gate_ref, act, dmix, dout, work, contrib,
        acc, snd, rcv,
        in_s, out_s, req_s, req_r, f_s, f_r, c_s, c_r, m_s, m_r, g_s, g_r, w_s, w_r,
    ) = refs
    shared = send_c is None
    send_c = send_f if shared else send_c
    loads = [
        pltpu.make_async_copy(source, target, in_s.at[i])
        for i, (source, target) in enumerate(
            zip(
                (feat_in, cot_in, wig_in, *weights_in),
                (feat_ref, cot_ref, wig_raw, fa0, fa1, fa2, sb0, sb1, sb2),
            )
        )
    ]
    for load in loads:
        load.start()
    C = LANES
    coefs, atoms, _ = feat_ref.shape
    half = coefs * C
    edges = wig_raw.shape[2]
    pair_rows = pf.shape[0]
    parts = tile_parts(coefs, width)
    starts = unique(p[2] for p in parts)
    offsets = own_offsets(coefs, width)
    kinds = unique(offsets)
    slots = peers * TILE
    me = lax.axis_index("atoms")

    barrier = pltpu.get_barrier_semaphore()

    def greet(k, carry):
        pl.semaphore_signal(barrier, inc=1, device_id=(lax.rem(me + k, peers),), device_id_type=MESH)
        return carry

    lax.fori_loop(1, peers, greet, 0)

    pairs = blocks_ref.shape[1]
    row_width = pair_rows_ref.shape[0]
    ranks = width // row_width
    owners = blocks_ref[...].astype(F32)
    earlier = lax.broadcasted_iota(jnp.int32, (pairs, pairs), 0) < lax.broadcasted_iota(
        jnp.int32, (pairs, pairs), 1
    )
    peer_ids = lax.broadcasted_iota(jnp.int32, (peers, pairs), 0).astype(F32)
    owned = [(peer_ids == owners[side : side + 1]).astype(F32) for side in (0, 1)]
    count = dot_nn((owned[0] + owned[1]).astype(BF16), as_hot(earlier))
    lane = lax.broadcasted_iota(jnp.int32, (row_width, C), 1)
    member = lax.broadcasted_iota(jnp.int32, (row_width, C), 0)

    def wanted_row(lanes):
        flat = lanes % TILE
        for s, start in enumerate(starts):
            flat = jnp.where(lanes // TILE == s, flat + start, flat)
        later = flat >= width
        return jnp.where(later, flat - width, flat), later

    row_at, _ = wanted_row(lane)
    lanes_all = lax.broadcasted_iota(jnp.int32, (peers, C), 1)
    _, second = wanted_row(lanes_all)
    request = jnp.where(second, float(atoms), 0.0)
    for k in range(ranks):
        choose = as_hot((row_at == member + k * row_width) & (lane < TILE * len(starts)))
        for side in (0, 1):
            rows = dot_tn(pair_rows_ref[:, side, :].astype(F32).astype(BF16), choose)
            holder = jnp.where(count == float(k), owned[side], 0.0)
            request = request + dot_nn(holder.astype(BF16), rows.astype(BF16))
    req_ref[...] = request.reshape(peers, 1, C)

    pl.semaphore_wait(barrier, peers - 1)

    def copies(source, target, send_sem, recv_sem):
        def at(k):
            to = lax.rem(me + k * STRIDE, peers)
            return pltpu.make_async_remote_copy(
                src_ref=source.at[to],
                dst_ref=target.at[me],
                send_sem=send_sem.at[k],
                recv_sem=recv_sem.at[k],
                device_id=(to,),
                device_id_type=MESH,
            )

        def start(first=1, last=peers):
            def go(k, carry):
                at(k).start()
                return carry

            lax.fori_loop(first, last, go, 0)

        def wait():
            def go(k, carry):
                at(k).wait()
                return carry

            lax.fori_loop(1, peers, go, 0)

        return start, wait

    start_req, wait_req = copies(req_ref, asked, req_s, req_r)
    start_req()
    asked[me] = req_ref[me]
    wait_req()

    rows_of = lax.broadcasted_iota(jnp.int32, (slots, peers), 0) // TILE
    chooser = as_hot(rows_of == lax.broadcasted_iota(jnp.int32, (slots, peers), 1))
    wanted = dot_nn(chooser, asked[...].reshape(peers, C).astype(BF16))
    slot_lane = lax.broadcasted_iota(jnp.int32, (slots, C), 1)
    inner = lax.broadcasted_iota(jnp.int32, (slots, C), 0) % TILE
    atom_ids = lax.broadcasted_iota(jnp.int32, (slots, 2 * atoms), 1).astype(F32)
    for s in range(len(starts)):
        column = jnp.sum(jnp.where(slot_lane == inner + s * TILE, wanted, 0.0), axis=1, keepdims=True)
        hots[s] = as_hot(column == atom_ids)

    def pick(block_ref, out_ref):
        for t, (first, last, start) in enumerate(parts):
            hot = hots.at[starts.index(start)]
            depth = (last - first + 1) * atoms
            table = block_ref[first : last + 1].reshape(depth, C)
            rows = dot_nn(hot[:, :depth], table).astype(BF16)
            out_ref[:, TILE * t : TILE * (t + 1), :] = rows.reshape(peers, TILE, C)

    start_f, wait_f = copies(send_f, recv_f, f_s, f_r)
    start_c, wait_c = copies(send_c, recv_c, c_s, c_r)
    loads[0].wait()
    pick(feat_ref, send_f)
    start_f()
    recv_f[me] = send_f[me]
    if shared:
        wait_f()
    loads[1].wait()
    pick(cot_ref, send_c)
    start_c()
    recv_c[me] = send_c[me]

    own = None
    end_row = lax.broadcasted_iota(jnp.int32, (pair_rows, pairs), 0)
    first_row = lax.broadcasted_iota(jnp.int32, (pair_rows, pairs), 1) * (2 * row_width)
    row_ids = lax.broadcasted_iota(jnp.int32, (8, pairs), 0)
    for side in (0, 1):
        low = first_row + side * row_width
        inside = (end_row >= low) & (end_row < low + row_width)
        shift = jnp.where(inside, end_row - low, 0)
        held = jnp.sum(owned[side] * count, axis=0, keepdims=True)
        known = jnp.where(row_ids == 0, owners[side : side + 1], jnp.where(row_ids == 1, held, 0.0))
        known = jnp.where(row_ids == 2, 1.0, known)
        term = lax.dot_general(
            as_hot(inside), known.astype(BF16), (((1,), (1,)), ((), ())), preferred_element_type=F32
        )
        term = jnp.concatenate(
            [term[:, :2], jnp.sum(shift.astype(F32), axis=1, keepdims=True)], axis=1
        )
        own = term if own is None else own + term
    in_slot = own[:, 1:2] * float(row_width) + own[:, 2:3]
    base = 0
    for off in kinds:
        tiles = 1 + (off + width - 1) // TILE
        place = in_slot + float(off)
        place = jnp.where(place >= float(TILE), place + float(slots - TILE), place)
        place = place + own[:, 0:1] * float(TILE)
        ids = lax.broadcasted_iota(jnp.int32, (pair_rows, tiles * slots), 1).astype(F32)
        mine[:, base : base + tiles * slots] = as_hot(place == ids)
        base += tiles * slots

    for load in loads[2:]:
        load.wait()
    diagonal = lax.broadcasted_iota(jnp.int32, (edges, edges), 0) == lax.broadcasted_iota(
        jnp.int32, (edges, edges), 1
    )
    unit = diagonal.astype(F32)
    for i in range(coefs):
        turned = lax.dot_general(
            unit, wig_raw[i], (((1,), (1,)), ((), ())),
            precision=lax.Precision.HIGHEST, preferred_element_type=F32,
        )
        wig_ref[:, i * coefs : (i + 1) * coefs] = turned
    ends = lax.dot_general(
        as_hot(diagonal), ends_ref[...].astype(F32).astype(BF16), (((1,), (1,)), ((), ())),
        preferred_element_type=F32,
    )
    pair_base = None
    edge_ids = lax.broadcasted_iota(jnp.int32, (edges, 1), 0)
    for p in range(edges // per_pair):
        step = jnp.where(edge_ids >= p * per_pair, float(2 * row_width), 0.0)
        if p and p % pair_chunk == 0:
            step = jnp.where(edge_ids >= p * per_pair, float(2 * row_width * (1 - pair_chunk)), 0.0)
        pair_base = jnp.zeros_like(step) if pair_base is None else pair_base + step
    pos_ref[...] = ends + pair_base + jnp.where(
        lax.broadcasted_iota(jnp.int32, (edges, 2), 1) == 1, float(row_width), 0.0
    )
    widen_into(wa1, fa1)
    widen_into(wa2, fa2)
    widen_into(wb1, sb1)
    widen_into(wb2, sb2)

    def own_hot(j):
        m = kinds.index(offsets[j])
        base = sum(slots * (1 + (off + width - 1) // TILE) for off in kinds[:m])
        tiles = 1 + (offsets[j] + width - 1) // TILE
        return base, tiles, width * j // TILE

    def gather(recv, out):
        for j in range(coefs):
            base, tiles, first = own_hot(j)
            total = None
            for h in range(tiles):
                hot = mine[:, base + h * slots : base + (h + 1) * slots]
                t = first + h
                rows = recv[:, TILE * t : TILE * (t + 1), :].reshape(slots, C)
                term = dot_nn(hot, rows)
                total = term if total is None else total + term
            out[:, j * C : (j + 1) * C] = total.astype(BF16)

    def scatter(sums, out):
        for t in range(len(parts)):
            total = None
            for j in range(parts[t][0], parts[t][1] + 1):
                base, tiles, first = own_hot(j)
                h = t - first
                assert 0 <= h < tiles
                hot = mine[:, base + h * slots : base + (h + 1) * slots]
                term = dot_tn(hot, sums[:, j * C : (j + 1) * C])
                total = term if total is None else total + term
            out[:, TILE * t : TILE * (t + 1), :] = total.astype(BF16).reshape(peers, TILE, C)

    chunk = pair_chunk * per_pair
    locals_ = pair_chunk * 2 * (pair_rows // (2 * (edges // per_pair)))
    T, S = slice(0, chunk), slice(chunk, 2 * chunk)

    def hot_of(index):
        span = pl.ds(pl.multiple_of(index * chunk, chunk), chunk)
        ids = lax.broadcasted_iota(jnp.int32, (chunk, locals_), 1).astype(F32)
        return jnp.concatenate(
            [as_hot(pos_ref[span, side : side + 1] == ids) for side in (0, 1)], axis=0
        )

    def table_of(ref, index):
        return ref.at[pl.ds(pl.multiple_of(index * locals_, locals_), locals_)]

    def entries(index):
        wig = wig_ref[pl.ds(pl.multiple_of(index * chunk, chunk), chunk), :]

        def entry(row, col):
            k = row * coefs + col
            return jnp.broadcast_to(wig[:, k : k + 1], (chunk, C))

        return entry

    def rotate(index, hot, table, put):
        rows = table_of(table, index)
        for c in range(0, half, 384):
            work[:, c : c + 384] = dot_nn(hot, rows[:, c : c + 384])
        entry = entries(index)
        for i, o in enumerate(COEF_ORDER):
            at_target = at_source = None
            for j in degree_of(o):
                w = entry(o, j)
                left = w * work[T, j * C : (j + 1) * C]
                right = w * work[S, j * C : (j + 1) * C]
                at_target = left if at_target is None else at_target + left
                at_source = right if at_source is None else at_source + right
            put(i, at_target.astype(BF16), at_source.astype(BF16))

    def unrotate(index, hot, take, out):
        entry = entries(index)
        for j in range(coefs):
            at_target = at_source = None
            for i, o in enumerate(COEF_ORDER):
                if o not in degree_of(j):
                    continue
                w = entry(o, j)
                left, right = take(i)
                left, right = w * left, w * right
                at_target = left if at_target is None else at_target + left
                at_source = right if at_source is None else at_source + right
            for row, value in ((0, at_target), (chunk, at_source)):
                contrib[row : row + chunk, j * C : (j + 1) * C] = value.astype(BF16)
        rows = table_of(out, index)
        for c in range(0, half, 384):
            rows[:, c : c + 384] = dot_tn(hot, contrib[:, c : c + 384]).astype(BF16)

    def all_rows(index):
        return pl.ds(pl.multiple_of(index * 2 * chunk, 2 * chunk), 2 * chunk)

    def forward(index, carry):
        hot = hot_of(index)
        zc, hc, gc, ac = (r.at[all_rows(index)] for r in (z, hid, gate_ref, act))

        def put(i, rt, rs):
            left = slice(2 * i * C, (2 * i + 1) * C)
            right = slice((2 * i + 1) * C, (2 * i + 2) * C)
            zc[T, left] = rs
            zc[T, right] = rt
            zc[S, left] = rt
            zc[S, right] = rs

        rotate(index, hot, pf, put)
        first = dot_nn(zc[:, : 6 * C], fa0[...])
        hc[:, : 3 * C] = first[:, : 3 * C]
        gc[...] = jax.nn.sigmoid(first[:, 3 * C :])
        hc[:, 3 * C : 7 * C] = dot_nn(zc[:, 6 * C : 14 * C], wa1[...])
        hc[:, 7 * C :] = dot_nn(zc[:, 14 * C :], wa2[...])
        gate = gc[...]
        h0 = hc[:, :C]
        ac[:, :C] = (h0 * jax.nn.sigmoid(h0)).astype(BF16)
        for k in range(1, 9):
            ac[:, k * C : (k + 1) * C] = (hc[:, k * C : (k + 1) * C] * gate).astype(BF16)
        work[:, : 3 * C] = dot_nn(ac[:, : 3 * C], sb0[...])
        work[:, 3 * C : 7 * C] = dot_nn(ac[:, 3 * C : 7 * C], wb1[...])
        work[:, 7 * C : 9 * C] = dot_nn(ac[:, 7 * C :], wb2[...])

        def take(i):
            col = slice(i * C, (i + 1) * C)
            return work[T, col], work[S, col]

        unrotate(index, hot, take, am)
        return carry

    def backward_first(index, carry):
        hot = hot_of(index)
        dc = dmix.at[all_rows(index)]

        def put(i, ct, cs):
            dc[T, i * C : (i + 1) * C] = ct
            dc[S, i * C : (i + 1) * C] = cs

        rotate(index, hot, pc, put)
        return carry

    def backward(index, carry):
        hc, gc, dc, oc = (r.at[all_rows(index)] for r in (hid, gate_ref, dmix, dout))
        dact = work
        dact[:, : 3 * C] = dot_nt(dc[:, : 3 * C], sb0[...])
        dact[:, 3 * C : 7 * C] = dot_nt(dc[:, 3 * C : 7 * C], wb1[...])
        dact[:, 7 * C : 9 * C] = dot_nt(dc[:, 7 * C :], wb2[...])
        gate = gc[...]
        h0 = hc[:, :C]
        head = jax.nn.sigmoid(h0)
        oc[:, :C] = (dact[:, :C] * head * (1.0 + h0 * (1.0 - head))).astype(BF16)
        grad_gate = None
        for k in range(1, 9):
            d = dact[:, k * C : (k + 1) * C]
            term = d * hc[:, k * C : (k + 1) * C]
            grad_gate = term if grad_gate is None else grad_gate + term
            at = k * C if k < 3 else (k + 1) * C
            oc[:, at : at + C] = (d * gate).astype(BF16)
        oc[:, 3 * C : 4 * C] = (grad_gate * gate * (1.0 - gate)).astype(BF16)
        return carry

    def inputs_grad(index, carry):
        hot = hot_of(index)
        oc = dout.at[all_rows(index)]
        work[:, : 6 * C] = dot_nt(oc[:, : 4 * C], fa0[...])
        work[:, 6 * C : 14 * C] = dot_nt(oc[:, 4 * C : 8 * C], wa1[...])
        work[:, 14 * C :] = dot_nt(oc[:, 8 * C :], wa2[...])
        advance(PER_PIECE)

        def take(i):
            left = slice(2 * i * C, (2 * i + 1) * C)
            right = slice((2 * i + 1) * C, (2 * i + 2) * C)
            return work[T, right] + work[S, left], work[T, left] + work[S, right]

        unrotate(index, hot, take, ag)
        return carry

    chunks = edges // chunk
    if not shared:
        wait_f()
    gather(recv_f, pf)
    lax.fori_loop(0, chunks, forward, 0)
    ret_m, ret_g = recv_f, recv_c
    start_m, wait_m = copies(ret_m, back_m, m_s, m_r)
    start_g, wait_g = copies(ret_g, back_g, g_s, g_r)
    scatter(am, ret_m)
    back_m[me] = ret_m[me]
    returns = [(start, k) for start in (start_m, start_g) for k in range(1, peers)]
    grads_ready = [False]
    portion = max(1, (peers - 1) // 31)

    def give(number):
        number *= portion
        while number > 0 and returns:
            start, first = returns[0]
            if start is start_g and not grads_ready[0]:
                return
            last = first
            while returns and returns[0][0] is start and last - first < number:
                last = returns.pop(0)[1] + 1
            start(first, last)
            number -= last - first

    give(M_FIRST)

    wait_c()
    give(M_PART)
    gather(recv_c, pc)
    lax.fori_loop(0, chunks, backward_first, 0)
    give(M_PART)

    blocks = acc.shape[0]
    bits = peers.bit_length() - 1
    stream = blocks // streams
    core = lax.rem(me, 2)
    strides = [2**b for b in range(bits)]
    if bits >= 3:
        strides[1] = 2 + 2 * core
        strides[2] = 4 - 2 * core
    low = [q * stream for q in range(streams)]

    def w_copy(source, target, q, stage, stride):
        bit = lax.rem(me // stride, 2)
        return pltpu.make_async_remote_copy(
            src_ref=source,
            dst_ref=target,
            send_sem=w_s.at[stage * streams + q],
            recv_sem=w_r.at[stage * streams + q],
            device_id=(me + stride * (1 - 2 * bit),),
            device_id_type=MESH,
        )

    def halve_start(q, stage):
        size = stream >> (stage + 1)
        bit = lax.rem(me // strides[stage], 2)
        sent = low[q] + (1 - bit) * size
        low[q] = low[q] + bit * size
        snd[pl.ds(sent, size)] = acc[pl.ds(sent, size)].astype(BF16)
        landing = q * stream + stream - 2 * size
        copy = w_copy(snd.at[pl.ds(sent, size)], rcv.at[pl.ds(landing, size)], q, stage, strides[stage])
        copy.start()
        return copy, size, landing

    def halve_end(q, stage, state):
        copy, size, landing = state
        copy.wait()
        kept = pl.ds(low[q], size)
        total = acc[kept] + rcv[landing : landing + size].astype(F32)
        if stage == bits - 1:
            fin[kept] = (total * grad_scale).astype(BF16)
        else:
            acc[kept] = total

    def double_start(q, stage):
        size = stream >> (stage + 1)
        here = fin.at[pl.ds(low[q], size)]
        copy = w_copy(here, here, q, bits + stage, strides[stage])
        copy.start()
        return copy, size

    def double_end(q, stage, state):
        copy, size = state
        copy.wait()
        bit = lax.rem(me // strides[stage], 2)
        low[q] = low[q] - bit * size

    states = [None] * streams
    pending = []
    events = sorted(
        ((q * GROUPS // streams * SKEW + s, q, s) for q in range(streams) for s in range(2 * bits)), reverse=True
    )

    def step(q, s):
        if s < bits:
            halve_end(q, s, states[q])
            states[q] = halve_start(q, s + 1) if s + 1 < bits else double_start(q, s)
        else:
            stage = 2 * bits - 1 - s
            double_end(q, stage, states[q])
            if stage:
                states[q] = double_start(q, stage - 1)
            else:
                span = pl.ds(q * stream, stream)
                pending.append(pltpu.make_async_copy(fin.at[span], fin_out.at[span], out_s.at[2 + q]))
                pending[-1].start()

    started = [0]

    def advance(number):
        for _ in range(number):
            if events and events[-1][1] < started[0]:
                _, q, s = events.pop()
                step(q, s)
                give(PER_EVENT)

    at = 0

    def put(value):
        nonlocal at
        height = value.shape[0]
        for col in range(0, value.shape[1], C):
            acc[at // TILE : (at + height) // TILE] = value[:, col : col + C].reshape(height // TILE, TILE, C)
            at += height
        begin()

    def begin():
        while started[0] < streams and (started[0] + 1) * stream * TILE <= at:
            states[started[0]] = halve_start(started[0], 0)
            started[0] += 1

    def weight_pair(left, right):
        rows, cols = left.shape[1] // 2, right.shape[1] // 2
        upper = dot_tn(left[:, :rows], right)
        lower = dot_tn(left[:, rows:], right)
        put(upper[:, :cols] + lower[:, cols:])
        put(upper[:, cols:] - lower[:, :cols])

    put(dot_tn(act[:, : 3 * C], dmix[:, : 3 * C]))
    weight_pair(act[:, 3 * C : 7 * C], dmix[:, 3 * C : 7 * C])
    weight_pair(act[:, 7 * C :], dmix[:, 7 * C :])
    give(M_PART)
    lax.fori_loop(0, chunks, backward, 0)
    give(M_PART)
    put(dot_tn(z[:, : 6 * C], dout[:, : 4 * C]))
    advance(PER_PIECE)
    weight_pair(z[:, 6 * C : 14 * C], dout[:, 4 * C : 8 * C])
    advance(PER_PIECE)
    weight_pair(z[:, 14 * C :], dout[:, 8 * C :])
    if at < blocks * TILE:
        acc[at // TILE :] = jnp.zeros((blocks - at // TILE, TILE, C), F32)
        at = blocks * TILE
        begin()

    for index in range(chunks):
        inputs_grad(index, 0)
        advance(PER_PIECE)
    scatter(ag, ret_g)
    back_g[me] = ret_g[me]
    grads_ready[0] = True
    advance(BEFORE)
    while returns:
        give(AT_ONCE)
        advance(PER_SEND)

    def collect(back, out, dtype):
        for j in range(coefs):
            total = None
            for t, (first, last, start) in enumerate(parts):
                if not first <= j <= last:
                    continue
                hot = hots.at[starts.index(start)][:, (j - first) * atoms : (j - first + 1) * atoms]
                rows = back[:, TILE * t : TILE * (t + 1), :].reshape(slots, C)
                term = dot_tn(hot, rows)
                total = term if total is None else total + term
            out[j] = total.astype(dtype)

    wait_m()
    collect(back_m, msg_ref, BF16)
    pending.append(pltpu.make_async_copy(msg_ref, msg_out, out_s.at[0]))
    pending[-1].start()
    advance(len(events))
    wait_g()
    collect(back_g, grad_ref, F32)
    pending.append(pltpu.make_async_copy(grad_ref, grad_out, out_s.at[1]))
    pending[-1].start()
    for copy in pending:
        copy.wait()


def local(features, cotangent, wigner, pair_blocks, pair_rows, edge_ends, *weights):
    peers = lax.axis_size("atoms")
    atoms, coefs, channels = features.shape
    pair_count = pair_blocks.shape[0]
    row_width = pair_rows.shape[1]
    edges = edge_ends.shape[1]
    per_pair = edges // pair_count
    slot_count = max(2, 4 * pair_count // peers)
    width = slot_count * row_width
    half = coefs * channels
    bits = peers.bit_length() - 1

    parts = tile_parts(coefs, width)
    starts = unique(p[2] for p in parts)
    kinds = unique(own_offsets(coefs, width))
    crowded = peers > 64
    pair_chunk = pair_count // (4 if crowded else 2)
    total_rows = sum(w.size for w in weights) // LANES
    streams = 4 if crowded else STREAMS
    unit = TILE * peers * streams
    packed_rows = -(-total_rows // unit) * unit
    rows = 2 * edges
    chunk_rows = 2 * pair_chunk * per_pair
    V, DMA = pltpu.VMEM, pltpu.SemaphoreType.DMA
    first_m0, first_m1, first_m2, second_m0, second_m1, second_m2 = weights
    wide = [(2 * w.shape[1], 2 * w.shape[2]) for w in (first_m1, first_m2, second_m1, second_m2)]
    slots = peers * TILE
    mine_width = sum(slots * (1 + (off + width - 1) // TILE) for off in kinds)
    block = (peers, TILE * len(parts), channels)
    end_count = 2 * pair_count * row_width
    packed_blocks = (packed_rows // TILE, TILE, LANES)
    scratch = [
        V((coefs, atoms, channels), BF16),
        V((coefs, atoms, channels), F32),
        V(packed_blocks, BF16),
        V((coefs, atoms, channels), BF16),
        V((coefs, atoms, channels), BF16),
        V((coefs, coefs, edges), F32),
        *[V(w.shape, BF16) for w in weights],
        *[V(shape, BF16) for shape in wide],
        V((peers, 1, LANES), F32),
        V((peers, 1, LANES), F32),
        V((len(starts), slots, 2 * atoms), BF16),
        V((end_count, mine_width), BF16),
        V((edges, coefs * coefs), F32),
        V((edges, 2), F32),
        *[V(block, BF16) for _ in range(5 if crowded else 6)],
        *[V((end_count, half), BF16) for _ in range(4)],
        V((rows, 2 * half), BF16),
        V((rows, half), F32),
        V((rows, channels), F32),
        V((rows, half), BF16),
        V((rows, half), BF16),
        V((rows, half + channels), BF16),
        V((chunk_rows, 2 * half), F32),
        V((chunk_rows, half), BF16),
        V(packed_blocks, F32),
        V(packed_blocks, BF16),
        V(packed_blocks, BF16),
        DMA((3 + len(weights),)),
        DMA((2 + streams,)),
        *[DMA((peers,)) for _ in range(10)],
        DMA((2 * bits * streams,)),
        DMA((2 * bits * streams,)),
    ]
    whole = pl.BlockSpec(memory_space=pltpu.VMEM)
    first_block = 15 + 3 + 9 + 4 + 6
    grad_scale = (2.0 * edges * peers) ** (-0.5)

    def body(*refs):
        refs = list(refs)
        if crowded:
            refs.insert(first_block + 1, None)
        main_kernel(width, pair_chunk, per_pair, grad_scale, peers, streams, *refs)

    anywhere = pl.BlockSpec(memory_space=pl.ANY)
    messages, grads, packed = pl.pallas_call(
        body,
        out_shape=[
            jax.ShapeDtypeStruct((coefs, atoms, channels), BF16),
            jax.ShapeDtypeStruct((coefs, atoms, channels), F32),
            jax.ShapeDtypeStruct(packed_blocks, BF16),
        ],
        in_specs=[anywhere] * (3 + len(weights)) + [whole] * 3,
        out_specs=[anywhere] * 3,
        scratch_shapes=scratch,
        compiler_params=pltpu.CompilerParams(
            collective_id=0, has_side_effects=True, vmem_limit_bytes=VMEM_BYTES
        ),
        name="edges",
    )(
        jnp.transpose(features, (1, 0, 2)), jnp.transpose(cotangent, (1, 0, 2)), wigner, *weights,
        jnp.transpose(pair_blocks), jnp.transpose(pair_rows, (1, 0, 2)), edge_ends,
    )
    ordered = (second_m0, second_m1, second_m2, first_m0, first_m1, first_m2)

    def final(*refs):
        final_kernel(len(ordered), *refs)

    shapes = [jax.ShapeDtypeStruct(w.shape, F32) for w in ordered]
    messages, grads, *outs = pl.pallas_call(
        final,
        out_shape=[
            jax.ShapeDtypeStruct(messages.shape, BF16), jax.ShapeDtypeStruct(grads.shape, F32), *shapes
        ],
        in_specs=[anywhere, whole, whole],
        out_specs=[anywhere] * (2 + len(ordered)),
        scratch_shapes=[
            *[V(w.shape, F32) for w in ordered], V(packed.shape, BF16), DMA((2 + 2 * len(ordered),))
        ],
        compiler_params=pltpu.CompilerParams(vmem_limit_bytes=VMEM_BYTES),
        name="finish",
    )(packed, messages, grads)
    outs = (*outs[3:], *outs[:3])
    return (jnp.transpose(messages, (1, 0, 2)), jnp.transpose(grads, (1, 0, 2)), *outs)


def solution(mesh):
    in_specs = (
        P("atoms", None, None),
        P("atoms", None, None),
        P(None, None, "atoms"),
        P("atoms", None),
        P(None, None, "atoms"),
        P(None, "atoms"),
        P(),
        P(),
        P(),
        P(),
        P(),
        P(),
    )
    out_specs = (P("atoms", None, None), P("atoms", None, None), P(), P(), P(), P(), P(), P())
    return jax.shard_map(local, mesh=mesh, in_specs=in_specs, out_specs=out_specs, check_vma=False)
```

```python
import jax
import jax.numpy as jnp
from jax import lax
from jax.experimental import pallas as pl
from jax.experimental.pallas import tpu as pltpu
from jax.sharding import PartitionSpec as P

COEF_ORDER = (0, 2, 6, 3, 7, 1, 5, 8, 4)
DEGREES = ((0, 1), (1, 4), (4, 9))
LANES = 128
TILE = 16
STREAMS = 8
STRIDE = 11
BEFORE = 0
SKEW = 0
PER_PIECE = 8
AT_ONCE = 1
PER_SEND = 1
PER_EVENT = 0
GROUPS = 2
M_FIRST = 31
M_PART = 4
VMEM_BYTES = 66_000_000
MESH = pl.DeviceIdType.MESH
F32, BF16 = jnp.float32, jnp.bfloat16


def degree_of(index):
    for low, high in DEGREES:
        if low <= index < high:
            return range(low, high)


def dot_nn(left, right):
    return jnp.dot(left, right, preferred_element_type=F32)


def dot_nt(left, right):
    return lax.dot_general(left, right, (((1,), (1,)), ((), ())), preferred_element_type=F32)


def dot_tn(left, right):
    return lax.dot_general(left, right, (((0,), (0,)), ((), ())), preferred_element_type=F32)


def as_hot(hit):
    return hit.astype(F32).astype(BF16)


def tile_parts(coefs, width):
    tiles = -(-coefs * width // TILE)
    parts = []
    for t in range(tiles):
        first = TILE * t // width
        last = min((TILE * t + TILE - 1) // width, coefs - 1)
        assert last - first <= 1
        parts.append((first, last, TILE * t % width))
    return parts


def own_offsets(coefs, width):
    return [width * j % TILE for j in range(coefs)]


def unique(values):
    return sorted(set(values))


def widen_into(ref, pair_ref):
    rows, cols = pair_ref.shape[1], pair_ref.shape[2]
    ref[:rows, :cols] = pair_ref[0]
    ref[:rows, cols:] = pair_ref[1]
    ref[rows:, :cols] = (-pair_ref[1].astype(F32)).astype(BF16)
    ref[rows:, cols:] = pair_ref[0]


def final_kernel(weight_count, packed_in, messages_ref, grads_ref, *refs):
    messages_out, grads_out = refs[:2]
    outs = refs[2 : 2 + weight_count]
    staged = refs[2 + weight_count : 2 + 2 * weight_count]
    packed_ref, sems = refs[-2:]
    loads = []
    at = 0
    for index, ref in enumerate(staged):
        blocks = ref.size // (TILE * LANES)
        span = pl.ds(at, blocks)
        loads.append(
            pltpu.make_async_copy(packed_in.at[span], packed_ref.at[span], sems.at[2 + weight_count + index])
        )
        loads[-1].start()
        at += blocks
    pending = [
        pltpu.make_async_copy(messages_ref, messages_out, sems.at[0]),
        pltpu.make_async_copy(grads_ref, grads_out, sems.at[1]),
    ]
    for copy in pending:
        copy.start()
    at = 0
    for index, (ref, out) in enumerate(zip(staged, outs)):
        loads[index].wait()
        views = [ref] if len(ref.shape) == 2 else [ref.at[0], ref.at[1]]
        for view in views:
            height, width = view.shape
            for col in range(0, width, LANES):
                rows = packed_ref[at // TILE : (at + height) // TILE]
                view[:, col : col + LANES] = rows.reshape(height, LANES).astype(F32)
                at += height
        copy = pltpu.make_async_copy(ref, out, sems.at[2 + index])
        copy.start()
        pending.append(copy)
    for copy in pending:
        copy.wait()


def main_kernel(width, pair_chunk, per_pair, grad_scale, peers, streams, *refs):
    (
        feat_in, cot_in, wig_in, *weights_in,
        blocks_ref, pair_rows_ref, ends_ref,
        msg_out, grad_out, fin_out,
        msg_ref, grad_ref, fin,
        feat_ref, cot_ref, wig_raw, fa0, fa1, fa2, sb0, sb1, sb2,
        wa1, wa2, wb1, wb2,
        req_ref, asked, hots, mine, wig_ref, pos_ref, send_f, send_c, recv_f, recv_c, back_m, back_g,
        pf, pc, am, ag,
        z, hid, gate_ref, act, dmix, dout, work, contrib,
        acc, snd, rcv,
        in_s, out_s, req_s, req_r, f_s, f_r, c_s, c_r, m_s, m_r, g_s, g_r, w_s, w_r,
    ) = refs
    shared = send_c is None
    send_c = send_f if shared else send_c
    loads = [
        pltpu.make_async_copy(source, target, in_s.at[i])
        for i, (source, target) in enumerate(
            zip(
                (feat_in, cot_in, wig_in, *weights_in),
                (feat_ref, cot_ref, wig_raw, fa0, fa1, fa2, sb0, sb1, sb2),
            )
        )
    ]
    for load in loads:
        load.start()
    C = LANES
    coefs, atoms, _ = feat_ref.shape
    half = coefs * C
    edges = wig_raw.shape[2]
    pair_rows = pf.shape[0]
    parts = tile_parts(coefs, width)
    starts = unique(p[2] for p in parts)
    offsets = own_offsets(coefs, width)
    kinds = unique(offsets)
    slots = peers * TILE
    me = lax.axis_index("atoms")

    barrier = pltpu.get_barrier_semaphore()

    def greet(k, carry):
        pl.semaphore_signal(barrier, inc=1, device_id=(lax.rem(me + k, peers),), device_id_type=MESH)
        return carry

    lax.fori_loop(1, peers, greet, 0)

    pairs = blocks_ref.shape[1]
    row_width = pair_rows_ref.shape[0]
    ranks = width // row_width
    owners = blocks_ref[...].astype(F32)
    earlier = lax.broadcasted_iota(jnp.int32, (pairs, pairs), 0) < lax.broadcasted_iota(
        jnp.int32, (pairs, pairs), 1
    )
    peer_ids = lax.broadcasted_iota(jnp.int32, (peers, pairs), 0).astype(F32)
    owned = [(peer_ids == owners[side : side + 1]).astype(F32) for side in (0, 1)]
    count = dot_nn((owned[0] + owned[1]).astype(BF16), as_hot(earlier))
    lane = lax.broadcasted_iota(jnp.int32, (row_width, C), 1)
    member = lax.broadcasted_iota(jnp.int32, (row_width, C), 0)

    def wanted_row(lanes):
        flat = lanes % TILE
        for s, start in enumerate(starts):
            flat = jnp.where(lanes // TILE == s, flat + start, flat)
        later = flat >= width
        return jnp.where(later, flat - width, flat), later

    row_at, _ = wanted_row(lane)
    lanes_all = lax.broadcasted_iota(jnp.int32, (peers, C), 1)
    _, second = wanted_row(lanes_all)
    request = jnp.where(second, float(atoms), 0.0)
    for k in range(ranks):
        choose = as_hot((row_at == member + k * row_width) & (lane < TILE * len(starts)))
        for side in (0, 1):
            rows = dot_tn(pair_rows_ref[:, side, :].astype(F32).astype(BF16), choose)
            holder = jnp.where(count == float(k), owned[side], 0.0)
            request = request + dot_nn(holder.astype(BF16), rows.astype(BF16))
    req_ref[...] = request.reshape(peers, 1, C)

    pl.semaphore_wait(barrier, peers - 1)

    def copies(source, target, send_sem, recv_sem):
        def at(k):
            to = lax.rem(me + k * STRIDE, peers)
            return pltpu.make_async_remote_copy(
                src_ref=source.at[to],
                dst_ref=target.at[me],
                send_sem=send_sem.at[k],
                recv_sem=recv_sem.at[k],
                device_id=(to,),
                device_id_type=MESH,
            )

        def start(first=1, last=peers):
            def go(k, carry):
                at(k).start()
                return carry

            lax.fori_loop(first, last, go, 0)

        def wait():
            def go(k, carry):
                at(k).wait()
                return carry

            lax.fori_loop(1, peers, go, 0)

        return start, wait

    start_req, wait_req = copies(req_ref, asked, req_s, req_r)
    start_req()
    asked[me] = req_ref[me]
    wait_req()

    rows_of = lax.broadcasted_iota(jnp.int32, (slots, peers), 0) // TILE
    chooser = as_hot(rows_of == lax.broadcasted_iota(jnp.int32, (slots, peers), 1))
    wanted = dot_nn(chooser, asked[...].reshape(peers, C).astype(BF16))
    slot_lane = lax.broadcasted_iota(jnp.int32, (slots, C), 1)
    inner = lax.broadcasted_iota(jnp.int32, (slots, C), 0) % TILE
    atom_ids = lax.broadcasted_iota(jnp.int32, (slots, 2 * atoms), 1).astype(F32)
    for s in range(len(starts)):
        column = jnp.sum(jnp.where(slot_lane == inner + s * TILE, wanted, 0.0), axis=1, keepdims=True)
        hots[s] = as_hot(column == atom_ids)

    def pick(block_ref, out_ref):
        for t, (first, last, start) in enumerate(parts):
            hot = hots.at[starts.index(start)]
            depth = (last - first + 1) * atoms
            table = block_ref[first : last + 1].reshape(depth, C)
            rows = dot_nn(hot[:, :depth], table).astype(BF16)
            out_ref[:, TILE * t : TILE * (t + 1), :] = rows.reshape(peers, TILE, C)

    start_f, wait_f = copies(send_f, recv_f, f_s, f_r)
    start_c, wait_c = copies(send_c, recv_c, c_s, c_r)
    loads[0].wait()
    pick(feat_ref, send_f)
    start_f()
    recv_f[me] = send_f[me]
    if shared:
        wait_f()
    loads[1].wait()
    pick(cot_ref, send_c)
    start_c()
    recv_c[me] = send_c[me]

    own = None
    end_row = lax.broadcasted_iota(jnp.int32, (pair_rows, pairs), 0)
    first_row = lax.broadcasted_iota(jnp.int32, (pair_rows, pairs), 1) * (2 * row_width)
    row_ids = lax.broadcasted_iota(jnp.int32, (8, pairs), 0)
    for side in (0, 1):
        low = first_row + side * row_width
        inside = (end_row >= low) & (end_row < low + row_width)
        shift = jnp.where(inside, end_row - low, 0)
        held = jnp.sum(owned[side] * count, axis=0, keepdims=True)
        known = jnp.where(row_ids == 0, owners[side : side + 1], jnp.where(row_ids == 1, held, 0.0))
        known = jnp.where(row_ids == 2, 1.0, known)
        term = lax.dot_general(
            as_hot(inside), known.astype(BF16), (((1,), (1,)), ((), ())), preferred_element_type=F32
        )
        term = jnp.concatenate(
            [term[:, :2], jnp.sum(shift.astype(F32), axis=1, keepdims=True)], axis=1
        )
        own = term if own is None else own + term
    in_slot = own[:, 1:2] * float(row_width) + own[:, 2:3]
    base = 0
    for off in kinds:
        tiles = 1 + (off + width - 1) // TILE
        place = in_slot + float(off)
        place = jnp.where(place >= float(TILE), place + float(slots - TILE), place)
        place = place + own[:, 0:1] * float(TILE)
        ids = lax.broadcasted_iota(jnp.int32, (pair_rows, tiles * slots), 1).astype(F32)
        mine[:, base : base + tiles * slots] = as_hot(place == ids)
        base += tiles * slots

    for load in loads[2:]:
        load.wait()
    diagonal = lax.broadcasted_iota(jnp.int32, (edges, edges), 0) == lax.broadcasted_iota(
        jnp.int32, (edges, edges), 1
    )
    unit = diagonal.astype(F32)
    for i in range(coefs):
        turned = lax.dot_general(
            unit, wig_raw[i], (((1,), (1,)), ((), ())),
            precision=lax.Precision.HIGHEST, preferred_element_type=F32,
        )
        wig_ref[:, i * coefs : (i + 1) * coefs] = turned
    ends = lax.dot_general(
        as_hot(diagonal), ends_ref[...].astype(F32).astype(BF16), (((1,), (1,)), ((), ())),
        preferred_element_type=F32,
    )
    pair_base = None
    edge_ids = lax.broadcasted_iota(jnp.int32, (edges, 1), 0)
    for p in range(edges // per_pair):
        step = jnp.where(edge_ids >= p * per_pair, float(2 * row_width), 0.0)
        if p and p % pair_chunk == 0:
            step = jnp.where(edge_ids >= p * per_pair, float(2 * row_width * (1 - pair_chunk)), 0.0)
        pair_base = jnp.zeros_like(step) if pair_base is None else pair_base + step
    pos_ref[...] = ends + pair_base + jnp.where(
        lax.broadcasted_iota(jnp.int32, (edges, 2), 1) == 1, float(row_width), 0.0
    )
    widen_into(wa1, fa1)
    widen_into(wa2, fa2)
    widen_into(wb1, sb1)
    widen_into(wb2, sb2)

    def own_hot(j):
        m = kinds.index(offsets[j])
        base = sum(slots * (1 + (off + width - 1) // TILE) for off in kinds[:m])
        tiles = 1 + (offsets[j] + width - 1) // TILE
        return base, tiles, width * j // TILE

    def gather(recv, out):
        for j in range(coefs):
            base, tiles, first = own_hot(j)
            total = None
            for h in range(tiles):
                hot = mine[:, base + h * slots : base + (h + 1) * slots]
                t = first + h
                rows = recv[:, TILE * t : TILE * (t + 1), :].reshape(slots, C)
                term = dot_nn(hot, rows)
                total = term if total is None else total + term
            out[:, j * C : (j + 1) * C] = total.astype(BF16)

    def scatter(sums, out):
        for t in range(len(parts)):
            total = None
            for j in range(parts[t][0], parts[t][1] + 1):
                base, tiles, first = own_hot(j)
                h = t - first
                assert 0 <= h < tiles
                hot = mine[:, base + h * slots : base + (h + 1) * slots]
                term = dot_tn(hot, sums[:, j * C : (j + 1) * C])
                total = term if total is None else total + term
            out[:, TILE * t : TILE * (t + 1), :] = total.astype(BF16).reshape(peers, TILE, C)

    chunk = pair_chunk * per_pair
    locals_ = pair_chunk * 2 * (pair_rows // (2 * (edges // per_pair)))
    T, S = slice(0, chunk), slice(chunk, 2 * chunk)

    def hot_of(index):
        span = pl.ds(pl.multiple_of(index * chunk, chunk), chunk)
        ids = lax.broadcasted_iota(jnp.int32, (chunk, locals_), 1).astype(F32)
        return jnp.concatenate(
            [as_hot(pos_ref[span, side : side + 1] == ids) for side in (0, 1)], axis=0
        )

    def table_of(ref, index):
        return ref.at[pl.ds(pl.multiple_of(index * locals_, locals_), locals_)]

    def entries(index):
        wig = wig_ref[pl.ds(pl.multiple_of(index * chunk, chunk), chunk), :]

        def entry(row, col):
            k = row * coefs + col
            return jnp.broadcast_to(wig[:, k : k + 1], (chunk, C))

        return entry

    def rotate(index, hot, table, put):
        rows = table_of(table, index)
        for c in range(0, half, 384):
            work[:, c : c + 384] = dot_nn(hot, rows[:, c : c + 384])
        entry = entries(index)
        for i, o in enumerate(COEF_ORDER):
            at_target = at_source = None
            for j in degree_of(o):
                w = entry(o, j)
                left = w * work[T, j * C : (j + 1) * C]
                right = w * work[S, j * C : (j + 1) * C]
                at_target = left if at_target is None else at_target + left
                at_source = right if at_source is None else at_source + right
            put(i, at_target.astype(BF16), at_source.astype(BF16))

    def unrotate(index, hot, take, out):
        entry = entries(index)
        for j in range(coefs):
            at_target = at_source = None
            for i, o in enumerate(COEF_ORDER):
                if o not in degree_of(j):
                    continue
                w = entry(o, j)
                left, right = take(i)
                left, right = w * left, w * right
                at_target = left if at_target is None else at_target + left
                at_source = right if at_source is None else at_source + right
            for row, value in ((0, at_target), (chunk, at_source)):
                contrib[row : row + chunk, j * C : (j + 1) * C] = value.astype(BF16)
        rows = table_of(out, index)
        for c in range(0, half, 384):
            rows[:, c : c + 384] = dot_tn(hot, contrib[:, c : c + 384]).astype(BF16)

    def all_rows(index):
        return pl.ds(pl.multiple_of(index * 2 * chunk, 2 * chunk), 2 * chunk)

    def forward(index, carry):
        hot = hot_of(index)
        zc, hc, gc, ac = (r.at[all_rows(index)] for r in (z, hid, gate_ref, act))

        def put(i, rt, rs):
            left = slice(2 * i * C, (2 * i + 1) * C)
            right = slice((2 * i + 1) * C, (2 * i + 2) * C)
            zc[T, left] = rs
            zc[T, right] = rt
            zc[S, left] = rt
            zc[S, right] = rs

        rotate(index, hot, pf, put)
        first = dot_nn(zc[:, : 6 * C], fa0[...])
        hc[:, : 3 * C] = first[:, : 3 * C]
        gc[...] = jax.nn.sigmoid(first[:, 3 * C :])
        hc[:, 3 * C : 7 * C] = dot_nn(zc[:, 6 * C : 14 * C], wa1[...])
        hc[:, 7 * C :] = dot_nn(zc[:, 14 * C :], wa2[...])
        gate = gc[...]
        h0 = hc[:, :C]
        ac[:, :C] = (h0 * jax.nn.sigmoid(h0)).astype(BF16)
        for k in range(1, 9):
            ac[:, k * C : (k + 1) * C] = (hc[:, k * C : (k + 1) * C] * gate).astype(BF16)
        work[:, : 3 * C] = dot_nn(ac[:, : 3 * C], sb0[...])
        work[:, 3 * C : 7 * C] = dot_nn(ac[:, 3 * C : 7 * C], wb1[...])
        work[:, 7 * C : 9 * C] = dot_nn(ac[:, 7 * C :], wb2[...])

        def take(i):
            col = slice(i * C, (i + 1) * C)
            return work[T, col], work[S, col]

        unrotate(index, hot, take, am)
        return carry

    def backward_first(index, carry):
        hot = hot_of(index)
        dc = dmix.at[all_rows(index)]

        def put(i, ct, cs):
            dc[T, i * C : (i + 1) * C] = ct
            dc[S, i * C : (i + 1) * C] = cs

        rotate(index, hot, pc, put)
        return carry

    def backward(index, carry):
        hc, gc, dc, oc = (r.at[all_rows(index)] for r in (hid, gate_ref, dmix, dout))
        dact = work
        dact[:, : 3 * C] = dot_nt(dc[:, : 3 * C], sb0[...])
        dact[:, 3 * C : 7 * C] = dot_nt(dc[:, 3 * C : 7 * C], wb1[...])
        dact[:, 7 * C : 9 * C] = dot_nt(dc[:, 7 * C :], wb2[...])
        gate = gc[...]
        h0 = hc[:, :C]
        head = jax.nn.sigmoid(h0)
        oc[:, :C] = (dact[:, :C] * head * (1.0 + h0 * (1.0 - head))).astype(BF16)
        grad_gate = None
        for k in range(1, 9):
            d = dact[:, k * C : (k + 1) * C]
            term = d * hc[:, k * C : (k + 1) * C]
            grad_gate = term if grad_gate is None else grad_gate + term
            at = k * C if k < 3 else (k + 1) * C
            oc[:, at : at + C] = (d * gate).astype(BF16)
        oc[:, 3 * C : 4 * C] = (grad_gate * gate * (1.0 - gate)).astype(BF16)
        return carry

    def inputs_grad(index, carry):
        hot = hot_of(index)
        oc = dout.at[all_rows(index)]
        work[:, : 6 * C] = dot_nt(oc[:, : 4 * C], fa0[...])
        work[:, 6 * C : 14 * C] = dot_nt(oc[:, 4 * C : 8 * C], wa1[...])
        work[:, 14 * C :] = dot_nt(oc[:, 8 * C :], wa2[...])
        advance(PER_PIECE)

        def take(i):
            left = slice(2 * i * C, (2 * i + 1) * C)
            right = slice((2 * i + 1) * C, (2 * i + 2) * C)
            return work[T, right] + work[S, left], work[T, left] + work[S, right]

        unrotate(index, hot, take, ag)
        return carry

    chunks = edges // chunk
    if not shared:
        wait_f()
    gather(recv_f, pf)
    lax.fori_loop(0, chunks, forward, 0)
    ret_m, ret_g = recv_f, recv_c
    start_m, wait_m = copies(ret_m, back_m, m_s, m_r)
    start_g, wait_g = copies(ret_g, back_g, g_s, g_r)
    scatter(am, ret_m)
    back_m[me] = ret_m[me]
    returns = [(start, k) for start in (start_m, start_g) for k in range(1, peers)]
    grads_ready = [False]
    portion = max(1, (peers - 1) // 31)

    def give(number):
        number *= portion
        while number > 0 and returns:
            start, first = returns[0]
            if start is start_g and not grads_ready[0]:
                return
            last = first
            while returns and returns[0][0] is start and last - first < number:
                last = returns.pop(0)[1] + 1
            start(first, last)
            number -= last - first

    give(M_FIRST)

    wait_c()
    give(M_PART)
    gather(recv_c, pc)
    lax.fori_loop(0, chunks, backward_first, 0)
    give(M_PART)

    blocks = acc.shape[0]
    bits = peers.bit_length() - 1
    stream = blocks // streams
    core = lax.rem(me, 2)
    strides = [2**b for b in range(bits)]
    if bits >= 3:
        strides[1] = 2 + 2 * core
        strides[2] = 4 - 2 * core
    low = [q * stream for q in range(streams)]

    def w_copy(source, target, q, stage, stride):
        bit = lax.rem(me // stride, 2)
        return pltpu.make_async_remote_copy(
            src_ref=source,
            dst_ref=target,
            send_sem=w_s.at[stage * streams + q],
            recv_sem=w_r.at[stage * streams + q],
            device_id=(me + stride * (1 - 2 * bit),),
            device_id_type=MESH,
        )

    def halve_start(q, stage):
        size = stream >> (stage + 1)
        bit = lax.rem(me // strides[stage], 2)
        sent = low[q] + (1 - bit) * size
        low[q] = low[q] + bit * size
        snd[pl.ds(sent, size)] = acc[pl.ds(sent, size)].astype(BF16)
        landing = q * stream + stream - 2 * size
        copy = w_copy(snd.at[pl.ds(sent, size)], rcv.at[pl.ds(landing, size)], q, stage, strides[stage])
        copy.start()
        return copy, size, landing

    def halve_end(q, stage, state):
        copy, size, landing = state
        copy.wait()
        kept = pl.ds(low[q], size)
        total = acc[kept] + rcv[landing : landing + size].astype(F32)
        if stage == bits - 1:
            fin[kept] = (total * grad_scale).astype(BF16)
        else:
            acc[kept] = total

    def double_start(q, stage):
        size = stream >> (stage + 1)
        here = fin.at[pl.ds(low[q], size)]
        copy = w_copy(here, here, q, bits + stage, strides[stage])
        copy.start()
        return copy, size

    def double_end(q, stage, state):
        copy, size = state
        copy.wait()
        bit = lax.rem(me // strides[stage], 2)
        low[q] = low[q] - bit * size

    states = [None] * streams
    pending = []
    events = sorted(
        ((q * GROUPS // streams * SKEW + s, q, s) for q in range(streams) for s in range(2 * bits)), reverse=True
    )

    def step(q, s):
        if s < bits:
            halve_end(q, s, states[q])
            states[q] = halve_start(q, s + 1) if s + 1 < bits else double_start(q, s)
        else:
            stage = 2 * bits - 1 - s
            double_end(q, stage, states[q])
            if stage:
                states[q] = double_start(q, stage - 1)
            else:
                span = pl.ds(q * stream, stream)
                pending.append(pltpu.make_async_copy(fin.at[span], fin_out.at[span], out_s.at[2 + q]))
                pending[-1].start()

    started = [0]

    def advance(number):
        for _ in range(number):
            if events and events[-1][1] < started[0]:
                _, q, s = events.pop()
                step(q, s)
                give(PER_EVENT)

    at = 0

    def put(value):
        nonlocal at
        height = value.shape[0]
        for col in range(0, value.shape[1], C):
            acc[at // TILE : (at + height) // TILE] = value[:, col : col + C].reshape(height // TILE, TILE, C)
            at += height
        begin()

    def begin():
        while started[0] < streams and (started[0] + 1) * stream * TILE <= at:
            states[started[0]] = halve_start(started[0], 0)
            started[0] += 1

    def weight_pair(left, right):
        rows, cols = left.shape[1] // 2, right.shape[1] // 2
        upper = dot_tn(left[:, :rows], right)
        lower = dot_tn(left[:, rows:], right)
        put(upper[:, :cols] + lower[:, cols:])
        put(upper[:, cols:] - lower[:, :cols])

    put(dot_tn(act[:, : 3 * C], dmix[:, : 3 * C]))
    weight_pair(act[:, 3 * C : 7 * C], dmix[:, 3 * C : 7 * C])
    weight_pair(act[:, 7 * C :], dmix[:, 7 * C :])
    give(M_PART)
    lax.fori_loop(0, chunks, backward, 0)
    give(M_PART)
    put(dot_tn(z[:, : 6 * C], dout[:, : 4 * C]))
    advance(PER_PIECE)
    weight_pair(z[:, 6 * C : 14 * C], dout[:, 4 * C : 8 * C])
    advance(PER_PIECE)
    weight_pair(z[:, 14 * C :], dout[:, 8 * C :])
    if at < blocks * TILE:
        acc[at // TILE :] = jnp.zeros((blocks - at // TILE, TILE, C), F32)
        at = blocks * TILE
        begin()

    for index in range(chunks):
        inputs_grad(index, 0)
        advance(PER_PIECE)
    scatter(ag, ret_g)
    back_g[me] = ret_g[me]
    def collect(back, out, dtype):
        for j in range(coefs):
            total = None
            for t, (first, last, start) in enumerate(parts):
                if not first <= j <= last:
                    continue
                hot = hots.at[starts.index(start)][:, (j - first) * atoms : (j - first + 1) * atoms]
                rows = back[:, TILE * t : TILE * (t + 1), :].reshape(slots, C)
                term = dot_tn(hot, rows)
                total = term if total is None else total + term
            out[j] = total.astype(dtype)

    grads_ready[0] = True
    advance(BEFORE)
    collected = False
    while returns:
        give(AT_ONCE)
        advance(PER_SEND)
        if not collected and len(returns) <= peers // 2:
            collected = True
            wait_m()
            collect(back_m, msg_ref, BF16)
            pending.append(pltpu.make_async_copy(msg_ref, msg_out, out_s.at[0]))
            pending[-1].start()
    advance(len(events))
    wait_g()
    collect(back_g, grad_ref, F32)
    pending.append(pltpu.make_async_copy(grad_ref, grad_out, out_s.at[1]))
    pending[-1].start()
    for copy in pending:
        copy.wait()


def local(features, cotangent, wigner, pair_blocks, pair_rows, edge_ends, *weights):
    peers = lax.axis_size("atoms")
    atoms, coefs, channels = features.shape
    pair_count = pair_blocks.shape[0]
    row_width = pair_rows.shape[1]
    edges = edge_ends.shape[1]
    per_pair = edges // pair_count
    slot_count = max(2, 4 * pair_count // peers)
    width = slot_count * row_width
    half = coefs * channels
    bits = peers.bit_length() - 1

    parts = tile_parts(coefs, width)
    starts = unique(p[2] for p in parts)
    kinds = unique(own_offsets(coefs, width))
    crowded = peers > 64
    pair_chunk = pair_count // (4 if crowded else 2)
    total_rows = sum(w.size for w in weights) // LANES
    streams = 4 if crowded else STREAMS
    unit = TILE * peers * streams
    packed_rows = -(-total_rows // unit) * unit
    rows = 2 * edges
    chunk_rows = 2 * pair_chunk * per_pair
    V, DMA = pltpu.VMEM, pltpu.SemaphoreType.DMA
    first_m0, first_m1, first_m2, second_m0, second_m1, second_m2 = weights
    wide = [(2 * w.shape[1], 2 * w.shape[2]) for w in (first_m1, first_m2, second_m1, second_m2)]
    slots = peers * TILE
    mine_width = sum(slots * (1 + (off + width - 1) // TILE) for off in kinds)
    block = (peers, TILE * len(parts), channels)
    end_count = 2 * pair_count * row_width
    packed_blocks = (packed_rows // TILE, TILE, LANES)
    scratch = [
        V((coefs, atoms, channels), BF16),
        V((coefs, atoms, channels), F32),
        V(packed_blocks, BF16),
        V((coefs, atoms, channels), BF16),
        V((coefs, atoms, channels), BF16),
        V((coefs, coefs, edges), F32),
        *[V(w.shape, BF16) for w in weights],
        *[V(shape, BF16) for shape in wide],
        V((peers, 1, LANES), F32),
        V((peers, 1, LANES), F32),
        V((len(starts), slots, 2 * atoms), BF16),
        V((end_count, mine_width), BF16),
        V((edges, coefs * coefs), F32),
        V((edges, 2), F32),
        *[V(block, BF16) for _ in range(5 if crowded else 6)],
        *[V((end_count, half), BF16) for _ in range(4)],
        V((rows, 2 * half), BF16),
        V((rows, half), F32),
        V((rows, channels), F32),
        V((rows, half), BF16),
        V((rows, half), BF16),
        V((rows, half + channels), BF16),
        V((chunk_rows, 2 * half), F32),
        V((chunk_rows, half), BF16),
        V(packed_blocks, F32),
        V(packed_blocks, BF16),
        V(packed_blocks, BF16),
        DMA((3 + len(weights),)),
        DMA((2 + streams,)),
        *[DMA((peers,)) for _ in range(10)],
        DMA((2 * bits * streams,)),
        DMA((2 * bits * streams,)),
    ]
    whole = pl.BlockSpec(memory_space=pltpu.VMEM)
    first_block = 15 + 3 + 9 + 4 + 6
    grad_scale = (2.0 * edges * peers) ** (-0.5)

    def body(*refs):
        refs = list(refs)
        if crowded:
            refs.insert(first_block + 1, None)
        main_kernel(width, pair_chunk, per_pair, grad_scale, peers, streams, *refs)

    anywhere = pl.BlockSpec(memory_space=pl.ANY)
    messages, grads, packed = pl.pallas_call(
        body,
        out_shape=[
            jax.ShapeDtypeStruct((coefs, atoms, channels), BF16),
            jax.ShapeDtypeStruct((coefs, atoms, channels), F32),
            jax.ShapeDtypeStruct(packed_blocks, BF16),
        ],
        in_specs=[anywhere] * (3 + len(weights)) + [whole] * 3,
        out_specs=[anywhere] * 3,
        scratch_shapes=scratch,
        compiler_params=pltpu.CompilerParams(
            collective_id=0, has_side_effects=True, vmem_limit_bytes=VMEM_BYTES
        ),
        name="edges",
    )(
        jnp.transpose(features, (1, 0, 2)), jnp.transpose(cotangent, (1, 0, 2)), wigner, *weights,
        jnp.transpose(pair_blocks), jnp.transpose(pair_rows, (1, 0, 2)), edge_ends,
    )
    ordered = (second_m0, second_m1, second_m2, first_m0, first_m1, first_m2)

    def final(*refs):
        final_kernel(len(ordered), *refs)

    shapes = [jax.ShapeDtypeStruct(w.shape, F32) for w in ordered]
    messages, grads, *outs = pl.pallas_call(
        final,
        out_shape=[
            jax.ShapeDtypeStruct(messages.shape, BF16), jax.ShapeDtypeStruct(grads.shape, F32), *shapes
        ],
        in_specs=[anywhere, whole, whole],
        out_specs=[anywhere] * (2 + len(ordered)),
        scratch_shapes=[
            *[V(w.shape, F32) for w in ordered], V(packed.shape, BF16), DMA((2 + 2 * len(ordered),))
        ],
        compiler_params=pltpu.CompilerParams(vmem_limit_bytes=VMEM_BYTES),
        name="finish",
    )(packed, messages, grads)
    outs = (*outs[3:], *outs[:3])
    return (jnp.transpose(messages, (1, 0, 2)), jnp.transpose(grads, (1, 0, 2)), *outs)


def solution(mesh):
    in_specs = (
        P("atoms", None, None),
        P("atoms", None, None),
        P(None, None, "atoms"),
        P("atoms", None),
        P(None, None, "atoms"),
        P(None, "atoms"),
        P(),
        P(),
        P(),
        P(),
        P(),
        P(),
    )
    out_specs = (P("atoms", None, None), P("atoms", None, None), P(), P(), P(), P(), P(), P())
    return jax.shard_map(local, mesh=mesh, in_specs=in_specs, out_specs=out_specs, check_vma=False)
```
